128 devices in a mesh: fsdp: 32 (over x, z, core), tensor: 4 (over y).
Axes of the slice: x: 4, y: 4, z: 4, core: 2. Of those that a mesh axis runs over, the one named last changes fastest.
Arguments:
- tokens: bfloat16 [24576, 8192], P('fsdp'), may hold values from -6 to 6
- weight: bfloat16 [8192, 8192], P('fsdp', 'tensor'), may hold values from -0.0625 to 0.0625
- momentum: float32 [8192, 8192], P('fsdp', 'tensor'), may hold values from -700 to 700
- gradient: bfloat16 [8192, 8192], P('fsdp', 'tensor'), may hold values from -6 to 6
- probes: float32 [32, 8192], P(None, 'tensor'), may hold values from -6 to 6
Outputs:
- activations: float32 [24576, 8192], P('fsdp', 'tensor')
- momentum_out: float32 [8192, 8192], P('fsdp', 'tensor')
- krylov_scaled: float32 [96, 96], replicated
The draws below stay inside these ranges and needn't reach their ends.
All inputs are finite; a program needn't handle non-finite values.
Results may differ from the reference program's by a relative error of at most 0.0029.
Values may be sent and summed in bfloat16 or wider, within the bound.
A program may use at most 192 MiB of HBM per device.

```python
import math
import jax
import jax.numpy as jnp
from jax import lax

D_IN = 8192
D_OUT = 8192
K = 32
STEPS = 3
POWER = 32
TOKENS = 24576


def draw_momentum(key, part):
    keys = jax.random.split(key, 3)
    row_scale = jnp.exp(jax.random.uniform(keys[0], (D_IN, 1), jnp.float32) * math.log(10.0))
    col_scale = jnp.exp(jax.random.uniform(keys[1], (1, D_OUT), jnp.float32) * math.log(10.0))
    row_place = jnp.arange(D_IN, dtype=jnp.float32).reshape(D_IN, 1) / D_IN
    col_place = jnp.arange(D_OUT, dtype=jnp.float32).reshape(1, D_OUT) / D_OUT
    row_ramp = jnp.exp(row_place * math.log(4.0))
    col_ramp = jnp.exp(col_place * math.log(4.0))
    noise = jax.random.truncated_normal(keys[2], -4.0, 4.0, (D_IN, D_OUT), jnp.float32)
    return 0.1 * noise * row_scale * col_scale * row_ramp * col_ramp


def shard_levels(key, dims, cuts, low, high):
    loudness = 1.0
    for axis_at, blocks in cuts:
        steps = jax.random.uniform(jax.random.fold_in(jax.random.fold_in(key, 6), axis_at), (blocks,), jnp.float32, low / len(cuts), high / len(cuts))
        loudness = loudness * jnp.repeat(jnp.exp(steps), dims[axis_at] // blocks).reshape((-1,) + (1,) * (len(dims) - 1 - axis_at))
    return loudness


def gaussian(stream_key, dims, width, bound, shards=(), kind=jnp.bfloat16):
    values = width * jax.random.normal(stream_key, dims, jnp.float32)
    if shards:
        values = values * shard_levels(stream_key, dims, shards, -0.22, 0.18)
    return jnp.clip(values, -bound, bound).astype(kind)


def setup_inputs(seed: int = 0) -> dict:
    key_list = jax.random.split(jax.random.key(seed), 6)
    tokens = gaussian(key_list[0], (TOKENS, D_IN), 1.0, 6.0, ((0, 32),))
    weight = gaussian(key_list[1], (D_IN, D_OUT), D_IN ** -0.5, 0.0625, ((0, 32), (1, 4)))
    momentum = draw_momentum(jax.random.fold_in(key_list[5], 71), 0)
    gradient = gaussian(key_list[3], (D_IN, D_OUT), 1.0, 6.0, ((0, 32), (1, 4)))
    probes = gaussian(key_list[4], (K, D_OUT), 1.0, 6.0, ((1, 4),), jnp.float32)
    return {"tokens": tokens, "weight": weight, "momentum": momentum, "gradient": gradient, "probes": probes}


highest = lax.Precision.HIGHEST
decay_factor = 0.9

def hdot(left, right):
    return jnp.dot(left.astype(jnp.float32), right.astype(jnp.float32), precision=highest, preferred_element_type=jnp.float32)

def orthonormal(block_mat, gram_mat):
    factor_low = jnp.linalg.cholesky(gram_mat)
    basis_next = jax.scipy.linalg.solve_triangular(factor_low, block_mat, lower=True)
    return (basis_next, factor_low)

def assemble(diag_blocks, low_factors):
    blk_width = diag_blocks[0].shape[0]
    total_size = len(diag_blocks) * blk_width
    krylov = jnp.zeros((total_size, total_size), jnp.float32)
    for position, diag_mat in enumerate(diag_blocks):
        first_at = position * blk_width
        krylov = krylov.at[first_at:first_at + blk_width, first_at:first_at + blk_width].set(diag_mat)
    for position, factor_low in enumerate(low_factors):
        first_at = position * blk_width
        second_at = first_at + blk_width
        krylov = krylov.at[second_at:second_at + blk_width, first_at:second_at].set(factor_low.T)
        krylov = krylov.at[first_at:second_at, second_at:second_at + blk_width].set(factor_low)
    return krylov

def top_value(krylov):

    def advance(position, vector):
        moved = hdot(krylov, vector)
        return moved / jnp.sqrt(jnp.sum(moved * moved))
    vector = lax.fori_loop(0, POWER, advance, jnp.ones((krylov.shape[0],), jnp.float32))
    return jnp.sum(vector * hdot(krylov, vector))

def reference(tokens, weight, momentum, gradient, probes):
    moment = decay_factor * momentum + gradient.astype(jnp.float32)
    basis_now, factor_first = orthonormal(probes, hdot(probes, probes.T))
    basis_prev = jnp.zeros_like(basis_now)
    low_prev = jnp.zeros((K, K), jnp.float32)
    diag_blocks = []
    low_factors = []
    for lanczos_step in range(STEPS):
        reduced = hdot(basis_now, moment.T)
        images = hdot(reduced, moment)
        diag_raw = hdot(basis_now, images.T)
        diag_mat = 0.5 * (diag_raw + diag_raw.T)
        diag_blocks.append(diag_mat)
        if lanczos_step + 1 < STEPS:
            residue = images - hdot(diag_mat, basis_now) - hdot(low_prev.T, basis_prev)
            basis_next, factor_low = orthonormal(residue, hdot(residue, residue.T))
            low_factors.append(factor_low)
            basis_prev, low_prev, basis_now = (basis_now, factor_low, basis_next)
    krylov = assemble(diag_blocks, low_factors)
    top = top_value(krylov)
    new_weight = (weight.astype(jnp.float32) - moment / jnp.sqrt(top)).astype(jnp.bfloat16)
    activations = jnp.dot(tokens.astype(jnp.float32), new_weight.astype(jnp.float32), preferred_element_type=jnp.float32)
    return (activations, moment, krylov / top)
```

```python
import jax
import jax.numpy as jnp
from jax import lax
from jax.sharding import PartitionSpec as P

STEPS = 3
SQUARINGS = 5

highest = lax.Precision.HIGHEST


def hdot(left, right):
    return jnp.dot(left, right, precision=highest, preferred_element_type=jnp.float32)


def hdot_t(left, right):
    return lax.dot_general(
        left, right, (((1,), (1,)), ((), ())), precision=highest, preferred_element_type=jnp.float32
    )


def assemble(diag_blocks, low_factors):
    zero = jnp.zeros_like(diag_blocks[0])
    rows = []
    count = len(diag_blocks)
    for row in range(count):
        blocks = []
        for col in range(count):
            if row == col:
                blocks.append(diag_blocks[row])
            elif row == col + 1:
                blocks.append(low_factors[col].T)
            elif col == row + 1:
                blocks.append(low_factors[row])
            else:
                blocks.append(zero)
        rows.append(jnp.concatenate(blocks, axis=1))
    return jnp.concatenate(rows, axis=0)


def top_value(krylov):
    power = krylov / jnp.max(jnp.abs(krylov))
    for _ in range(SQUARINGS):
        power = hdot(power, power)
        power = power / jnp.max(jnp.abs(power))
    vector = jnp.sum(power, axis=1)
    vector = vector / jnp.sqrt(jnp.sum(vector * vector))
    return jnp.sum(vector * hdot(krylov, vector))


def local(tokens, weight, momentum, gradient, probes):
    moment = 0.9 * momentum + gradient.astype(jnp.float32)
    block = probes
    basis_prev = jnp.zeros_like(probes)
    diag_blocks = []
    low_factors = []
    for step in range(STEPS):
        product, gram = lax.psum((hdot_t(block, moment), hdot_t(block, block)), "tensor")
        low = jnp.linalg.cholesky(gram)
        reduced = jax.scipy.linalg.solve_triangular(low, product, lower=True)
        if step:
            low_factors.append(low)
        diag_part = hdot_t(reduced, reduced)
        if step + 1 < STEPS:
            basis = jax.scipy.linalg.solve_triangular(low, block, lower=True)
            images, diag_mat = lax.psum((hdot(reduced, moment), diag_part), "fsdp")
            residue = images - hdot(diag_mat, basis)
            if step:
                residue = residue - hdot(low.T, basis_prev)
            basis_prev, block = basis, residue
        else:
            diag_mat = lax.psum(diag_part, "fsdp")
        diag_blocks.append(0.5 * (diag_mat + diag_mat.T))
    krylov = assemble(diag_blocks, low_factors)
    top = top_value(krylov)
    new_weight = (weight.astype(jnp.float32) - moment / jnp.sqrt(top)).astype(jnp.bfloat16)
    summed = jnp.dot(
        tokens,
        lax.all_gather(new_weight, "fsdp", axis=0, tiled=True),
        preferred_element_type=jnp.float32,
    )
    return (summed, moment, krylov / top)


def solution(mesh):
    return jax.shard_map(
        local,
        mesh=mesh,
        in_specs=(
            P("fsdp", None),
            P("fsdp", "tensor"),
            P("fsdp", "tensor"),
            P("fsdp", "tensor"),
            P(None, "tensor"),
        ),
        out_specs=(P("fsdp", "tensor"), P("fsdp", "tensor"), P()),
        check_vma=False,
    )
```

```python
import functools

import jax
import jax.numpy as jnp
from jax import lax
from jax.experimental import pallas as pl
from jax.experimental.pallas import tpu as pltpu
from jax.sharding import PartitionSpec as P

STEPS = 3
K = 32
LANES = 128
HIGHEST = lax.Precision.HIGHEST
F32 = jnp.float32


def hdot(left, right):
    return jnp.dot(left, right, precision=HIGHEST, preferred_element_type=F32)


def hdot_t(left, right):
    return lax.dot_general(
        left, right, (((1,), (1,)), ((), ())), precision=HIGHEST, preferred_element_type=F32
    )


def eliminate(gram):
    lane = lax.broadcasted_iota(jnp.int32, (8, LANES), 1)
    sub = lax.broadcasted_iota(jnp.int32, (8, LANES), 0)
    sub_col = lax.broadcasted_iota(jnp.int32, (8, 1), 0)
    count = K // 8
    blocks = []
    for at in range(count):
        eye = jnp.where(lane == sub + (8 * at + K), 1.0, 0.0)
        blocks.append(gram[8 * at : 8 * at + 8, :] + eye)
    for j in range(K):
        at, row = divmod(j, 8)
        pivot_row = blocks[at][row : row + 1, :]
        inverse = 1.0 / blocks[at][row : row + 1, j : j + 1]
        scaled = pivot_row * inverse
        for other in range(at, count):
            column = blocks[other][:, j : j + 1]
            if other == at:
                column = jnp.where(sub_col > row, column, 0.0)
            blocks[other] = blocks[other] - column * scaled
    upper, inverse_low = [], []
    for at in range(count):
        row = sub + 8 * at
        pivots = jnp.sum(jnp.where(lane == row, blocks[at], 0.0), axis=1, keepdims=True)
        scaled = blocks[at] / jnp.sqrt(pivots)
        upper.append(jnp.where((lane >= row) & (lane < K), scaled, 0.0))
        shifted = pltpu.roll(scaled, LANES - K, 1)
        inverse_low.append(jnp.where(lane <= row, shifted, 0.0))
    return jnp.concatenate(upper, axis=0), jnp.concatenate(inverse_low, axis=0)


def pack(square):
    tile = square[0:8, :]
    for at in range(1, K // 8):
        tile = tile + pltpu.roll(square[8 * at : 8 * at + 8, :], K * at, 1)
    return tile


def unpack(tile):
    lane = lax.broadcasted_iota(jnp.int32, (8, LANES), 1)
    parts = []
    for at in range(K // 8):
        part = tile if at == 0 else pltpu.roll(tile, LANES - K * at, 1)
        parts.append(jnp.where(lane < K, part, 0.0))
    return jnp.concatenate(parts, axis=0)


def top_value(krylov):
    def unit(power):
        return power / jnp.max(jnp.abs(power))

    power = unit(krylov)
    for turn in range(5):
        power = hdot(power, power)
        if turn == 2:
            power = unit(power)
    down = jnp.sum(power, axis=1, keepdims=True)
    along = jnp.sum(power, axis=0, keepdims=True)
    length = jnp.sqrt(jnp.sum(down * down)) * jnp.sqrt(jnp.sum(along * along))
    return jnp.sum(krylov * (down * along)) / length


def lanczos_kernel(
    nf,
    nt,
    probes_ref,
    moment_ref,
    krylov_ref,
    scale_ref,
    block,
    basis,
    small,
    tbuf,
    fsend,
    frecv,
    gathered,
    drecv,
    t_send,
    t_recv,
    rs_send,
    rs_recv,
    ag_send,
    ag_recv,
    d_send,
    d_recv,
):
    mf = lax.axis_index("fsdp")
    mt = lax.axis_index("tensor")
    rows = moment_ref.shape[0]
    cols = moment_ref.shape[1]
    width = cols // 8

    def fsdp_at(k):
        return {"fsdp": lax.rem(mf + k, nf)}

    def tensor_at(k):
        return {"tensor": lax.rem(mt + k, nt)}

    barrier = pltpu.get_barrier_semaphore()

    @pl.loop(1, nf)
    def _(k):
        pl.semaphore_signal(barrier, inc=1, device_id=fsdp_at(k))

    @pl.loop(1, nt)
    def _(k):
        pl.semaphore_signal(barrier, inc=1, device_id=tensor_at(k))

    lane = lax.broadcasted_iota(jnp.int32, (K, LANES), 1)

    def to_all(src, dst, send, recv):
        @pl.loop(1, nf)
        def _(k):
            pltpu.make_async_remote_copy(
                src_ref=src(lax.rem(mf + k, nf)),
                dst_ref=dst,
                send_sem=send,
                recv_sem=recv,
                device_id=fsdp_at(k),
            ).start()

    def all_of(ref, send, recv, count):
        return pltpu.make_async_remote_copy(
            src_ref=ref.at[pl.ds(0, count)],
            dst_ref=ref.at[pl.ds(0, count)],
            send_sem=send,
            recv_sem=recv,
            device_id=fsdp_at(1),
        )

    block[...] = probes_ref[...]
    small[...] = jnp.zeros_like(small)
    upper = None
    diags, uppers = [], []
    for step in range(STEPS):
        now = block[...]
        mine = tbuf.at[step, mt]
        mine[:, rows:] = jnp.zeros((K, LANES), F32)
        mine[:, :rows] = hdot_t(now, moment_ref[...])
        mine[:, rows : rows + K] = hdot_t(now, now)
        if step == 0:
            pl.semaphore_wait(barrier, nf + nt - 2)

        @pl.loop(1, nt)
        def _(k):
            pltpu.make_async_remote_copy(
                src_ref=tbuf.at[step, mt],
                dst_ref=tbuf.at[step, mt],
                send_sem=t_send.at[step],
                recv_sem=t_recv.at[step],
                device_id=tensor_at(k),
            ).start()

        all_of(tbuf.at[step], t_send.at[step], t_recv.at[step], nt - 1).wait_recv()
        total = tbuf[step, 0]
        for other in range(1, nt):
            total = total + tbuf[step, other]
        upper_next, inverse_low = eliminate(total[:, rows:])
        if step:
            uppers.append(upper_next)
        inverse_low = inverse_low[:, :K]
        reduced = hdot(inverse_low, total[:, :rows])
        small[:, :K] = hdot_t(reduced, reduced)
        tile = pack(small[...])
        if step + 1 < STEPS:
            images = hdot(reduced, moment_ref[...])
            for r in range(4):
                for c in range(8):
                    fsend[step, 8 * r + c, :, :width] = images[
                        8 * r : 8 * r + 8, width * c : width * (c + 1)
                    ]
                    fsend[step, 8 * r + c, :, width:] = tile
            frecv[step, mf] = fsend[step, mf]
            to_all(
                lambda dest: fsend.at[step, dest],
                frecv.at[step, mf],
                rs_send.at[step],
                rs_recv.at[step],
            )
            basis[step] = hdot(inverse_low, now)
            all_of(frecv.at[step], rs_send.at[step], rs_recv.at[step], nf - 1).wait_recv()
            summed = jnp.sum(frecv[step], axis=0)
            gathered[step, mf] = summed[:, :width]
            to_all(
                lambda dest: gathered.at[step, mf],
                gathered.at[step, mf],
                ag_send.at[step],
                ag_recv.at[step],
            )
            diag = unpack(summed[:, width:])
            rest = hdot(diag[:, :K], basis[step])
            if step:
                rest = rest + hdot(upper_next[:, :K], basis[step - 1])
            block[...] = rest
            all_of(gathered.at[step], ag_send.at[step], ag_recv.at[step], nf - 1).wait_recv()
            for r in range(4):
                for c in range(8):
                    where = (slice(8 * r, 8 * r + 8), slice(width * c, width * (c + 1)))
                    block[where] = gathered[step, 8 * r + c] - block[where]
        else:
            drecv[mf] = tile
            to_all(lambda dest: drecv.at[mf], drecv.at[mf], d_send, d_recv)
            all_of(drecv, d_send, d_recv, nf - 1).wait_recv()
            diag = unpack(jnp.sum(drecv[...], axis=0))
        diags.append(diag)

    eye = jnp.where(lax.broadcasted_iota(jnp.int32, (K, K), 0) == lax.broadcasted_iota(jnp.int32, (K, K), 1), 1.0, 0.0)
    lows = []
    for at in range(STEPS - 1):
        small[:, :K] = hdot_t(eye, uppers[at][:, :K])
        lows.append(small[...])
    bands = []
    for at in range(STEPS):
        band = pltpu.roll(diags[at], K * at, 1) if at else diags[at]
        if at + 1 < STEPS:
            band = band + pltpu.roll(lows[at], K * (at + 1), 1)
        if at:
            before = uppers[at - 1]
            band = band + (pltpu.roll(before, K * (at - 1), 1) if at > 1 else before)
        bands.append(band)
    bands.append(jnp.zeros((K, LANES), F32))
    krylov = jnp.concatenate(bands, axis=0)
    top = top_value(krylov)
    krylov_ref[...] = krylov / top
    scale_ref[...] = jnp.full(scale_ref.shape, 1.0, F32) / jnp.sqrt(top)

    for step in range(STEPS):
        all_of(tbuf.at[step], t_send.at[step], t_recv.at[step], nt - 1).wait_send()
        if step + 1 < STEPS:
            all_of(fsend.at[step], rs_send.at[step], rs_recv.at[step], nf - 1).wait_send()
            all_of(gathered.at[step], ag_send.at[step], ag_recv.at[step], nf - 1).wait_send()
    all_of(drecv, d_send, d_recv, nf - 1).wait_send()


def lanczos(probes, moment, nf, nt):
    rows, cols = moment.shape
    width = cols // 8
    vmem = pl.BlockSpec(memory_space=pltpu.VMEM)
    dma = pltpu.SemaphoreType.DMA
    return pl.pallas_call(
        functools.partial(lanczos_kernel, nf, nt),
        out_shape=(
            jax.ShapeDtypeStruct((LANES, LANES), F32),
            jax.ShapeDtypeStruct((8, LANES), F32),
        ),
        in_specs=[vmem, vmem],
        out_specs=(vmem, vmem),
        scratch_shapes=[
            pltpu.VMEM((K, cols), F32),
            pltpu.VMEM((STEPS - 1, K, cols), F32),
            pltpu.VMEM((K, LANES), F32),
            pltpu.VMEM((STEPS, nt, K, rows + LANES), F32),
            pltpu.VMEM((STEPS - 1, nf, 8, width + LANES), F32),
            pltpu.VMEM((STEPS - 1, nf, 8, width + LANES), F32),
            pltpu.VMEM((STEPS - 1, nf, 8, width), F32),
            pltpu.VMEM((nf, 8, LANES), F32),
            dma((STEPS,)),
            dma((STEPS,)),
            dma((STEPS - 1,)),
            dma((STEPS - 1,)),
            dma((STEPS - 1,)),
            dma((STEPS - 1,)),
            dma(()),
            dma(()),
        ],
        compiler_params=pltpu.CompilerParams(
            collective_id=0, has_side_effects=True, vmem_limit_bytes=40 * 1024 * 1024
        ),
    )(probes, moment)


def local(nf, nt, tokens, weight, momentum, gradient, probes):
    moment = 0.9 * momentum + gradient.astype(F32)
    krylov, scale = lanczos(probes, moment, nf, nt)
    new_weight = (weight.astype(F32) - moment * scale[0, 0]).astype(jnp.bfloat16)
    summed = jnp.dot(
        tokens,
        lax.all_gather(new_weight, "fsdp", axis=0, tiled=True),
        preferred_element_type=F32,
    )
    size = STEPS * K
    return (summed, moment, krylov[:size, :size])


def solution(mesh):
    return jax.shard_map(
        functools.partial(local, mesh.shape["fsdp"], mesh.shape["tensor"]),
        mesh=mesh,
        in_specs=(
            P("fsdp", None),
            P("fsdp", "tensor"),
            P("fsdp", "tensor"),
            P("fsdp", "tensor"),
            P(None, "tensor"),
        ),
        out_specs=(P("fsdp", "tensor"), P("fsdp", "tensor"), P()),
        check_vma=False,
    )
```

```python
import functools

import jax
import jax.numpy as jnp
from jax import lax
from jax.experimental import pallas as pl
from jax.experimental.pallas import tpu as pltpu
from jax.sharding import PartitionSpec as P

STEPS = 3
K = 32
LANES = 128
HIGHEST = lax.Precision.HIGHEST
F32 = jnp.float32


def hdot(left, right):
    return jnp.dot(left, right, precision=HIGHEST, preferred_element_type=F32)


def hdot_t(left, right):
    return lax.dot_general(
        left, right, (((1,), (1,)), ((), ())), precision=HIGHEST, preferred_element_type=F32
    )


def eliminate(gram):
    lane = lax.broadcasted_iota(jnp.int32, (8, LANES), 1)
    sub = lax.broadcasted_iota(jnp.int32, (8, LANES), 0)
    sub_col = lax.broadcasted_iota(jnp.int32, (8, 1), 0)
    count = K // 8
    blocks = []
    for at in range(count):
        eye = jnp.where(lane == sub + (8 * at + K), 1.0, 0.0)
        blocks.append(gram[8 * at : 8 * at + 8, :] + eye)
    for j in range(K):
        at, row = divmod(j, 8)
        pivot_row = blocks[at][row : row + 1, :]
        inverse = 1.0 / blocks[at][row : row + 1, j : j + 1]
        scaled = pivot_row * inverse
        for other in range(at, count):
            column = blocks[other][:, j : j + 1]
            if other == at:
                column = jnp.where(sub_col > row, column, 0.0)
            blocks[other] = blocks[other] - column * scaled
    upper, inverse_low = [], []
    for at in range(count):
        row = sub + 8 * at
        pivots = jnp.sum(jnp.where(lane == row, blocks[at], 0.0), axis=1, keepdims=True)
        scaled = blocks[at] / jnp.sqrt(pivots)
        upper.append(jnp.where((lane >= row) & (lane < K), scaled, 0.0))
        shifted = pltpu.roll(scaled, LANES - K, 1)
        inverse_low.append(jnp.where(lane <= row, shifted, 0.0))
    return jnp.concatenate(upper, axis=0), jnp.concatenate(inverse_low, axis=0)


def pack(square):
    tile = square[0:8, :]
    for at in range(1, K // 8):
        tile = tile + pltpu.roll(square[8 * at : 8 * at + 8, :], K * at, 1)
    return tile


def unpack(tile):
    lane = lax.broadcasted_iota(jnp.int32, (8, LANES), 1)
    parts = []
    for at in range(K // 8):
        part = tile if at == 0 else pltpu.roll(tile, LANES - K * at, 1)
        parts.append(jnp.where(lane < K, part, 0.0))
    return jnp.concatenate(parts, axis=0)


def top_value(krylov):
    def unit(power):
        return power / jnp.max(jnp.abs(power))

    power = unit(krylov)
    for turn in range(5):
        power = hdot(power, power)
        if turn == 2:
            power = unit(power)
    down = jnp.sum(power, axis=1, keepdims=True)
    along = jnp.sum(power, axis=0, keepdims=True)
    length = jnp.sqrt(jnp.sum(down * down)) * jnp.sqrt(jnp.sum(along * along))
    return jnp.sum(krylov * (down * along)) / length


def lanczos_kernel(
    nf,
    nt,
    probes_ref,
    moment_ref,
    krylov_ref,
    scale_ref,
    block,
    basis,
    small,
    tbuf,
    fsend,
    frecv,
    gathered,
    drecv,
    t_send,
    t_recv,
    rs_send,
    rs_recv,
    ag_send,
    ag_recv,
    d_send,
    d_recv,
):
    mf = lax.axis_index("fsdp")
    mt = lax.axis_index("tensor")
    rows = moment_ref.shape[0]
    cols = moment_ref.shape[1]
    width = cols // 8

    def fsdp_at(k):
        return {"fsdp": lax.rem(mf + k, nf)}

    def tensor_at(k):
        return {"tensor": lax.rem(mt + k, nt)}

    barrier = pltpu.get_barrier_semaphore()

    @pl.loop(1, nf)
    def _(k):
        pl.semaphore_signal(barrier, inc=1, device_id=fsdp_at(k))

    @pl.loop(1, nt)
    def _(k):
        pl.semaphore_signal(barrier, inc=1, device_id=tensor_at(k))

    lane = lax.broadcasted_iota(jnp.int32, (K, LANES), 1)

    def to_all(src, dst, send, recv):
        @pl.loop(1, nf)
        def _(k):
            pltpu.make_async_remote_copy(
                src_ref=src(lax.rem(mf + k, nf)),
                dst_ref=dst,
                send_sem=send,
                recv_sem=recv,
                device_id=fsdp_at(k),
            ).start()

    def all_of(ref, send, recv, count):
        return pltpu.make_async_remote_copy(
            src_ref=ref.at[pl.ds(0, count)],
            dst_ref=ref.at[pl.ds(0, count)],
            send_sem=send,
            recv_sem=recv,
            device_id=fsdp_at(1),
        )

    block[...] = probes_ref[...]
    small[...] = jnp.zeros_like(small)
    upper = None
    diags, uppers = [], []
    for step in range(STEPS):
        now = block[...]
        mine = tbuf.at[step, mt]
        mine[:, rows:] = jnp.zeros((K, LANES), F32)
        mine[:, :rows] = hdot_t(now, moment_ref[...])
        mine[:, rows : rows + K] = hdot_t(now, now)
        if step == 0:
            pl.semaphore_wait(barrier, nf + nt - 2)

        @pl.loop(1, nt)
        def _(k):
            pltpu.make_async_remote_copy(
                src_ref=tbuf.at[step, mt],
                dst_ref=tbuf.at[step, mt],
                send_sem=t_send.at[step],
                recv_sem=t_recv.at[step],
                device_id=tensor_at(k),
            ).start()

        all_of(tbuf.at[step], t_send.at[step], t_recv.at[step], nt - 1).wait_recv()
        total = tbuf[step, 0]
        for other in range(1, nt):
            total = total + tbuf[step, other]
        upper_next, inverse_low = eliminate(total[:, rows:])
        if step:
            uppers.append(upper_next)
        inverse_low = inverse_low[:, :K]
        reduced = hdot(inverse_low, total[:, :rows])
        small[:, :K] = hdot_t(reduced, reduced)
        tile = pack(small[...])
        if step + 1 < STEPS:
            images = hdot(reduced, moment_ref[...])
            for r in range(4):
                for c in range(8):
                    fsend[step, 8 * r + c, :, :width] = images[
                        8 * r : 8 * r + 8, width * c : width * (c + 1)
                    ]
                    fsend[step, 8 * r + c, :, width:] = tile
            frecv[step, mf] = fsend[step, mf]
            to_all(
                lambda dest: fsend.at[step, dest],
                frecv.at[step, mf],
                rs_send.at[step],
                rs_recv.at[step],
            )
            basis[step] = hdot(inverse_low, now)
            all_of(frecv.at[step], rs_send.at[step], rs_recv.at[step], nf - 1).wait_recv()
            summed = jnp.sum(frecv[step], axis=0)
            gathered[step, mf] = summed[:, :width]
            to_all(
                lambda dest: gathered.at[step, mf],
                gathered.at[step, mf],
                ag_send.at[step],
                ag_recv.at[step],
            )
            diag = unpack(summed[:, width:])
            rest = hdot(diag[:, :K], basis[step])
            if step:
                rest = rest + hdot(upper_next[:, :K], basis[step - 1])
            block[...] = rest
            all_of(gathered.at[step], ag_send.at[step], ag_recv.at[step], nf - 1).wait_recv()
            for r in range(4):
                for c in range(8):
                    where = (slice(8 * r, 8 * r + 8), slice(width * c, width * (c + 1)))
                    block[where] = gathered[step, 8 * r + c] - block[where]
        else:
            drecv[mf] = tile
            to_all(lambda dest: drecv.at[mf], drecv.at[mf], d_send, d_recv)
            all_of(drecv, d_send, d_recv, nf - 1).wait_recv()
            diag = unpack(jnp.sum(drecv[...], axis=0))
        diags.append(diag)

    eye = jnp.where(lax.broadcasted_iota(jnp.int32, (K, K), 0) == lax.broadcasted_iota(jnp.int32, (K, K), 1), 1.0, 0.0)
    lows = []
    for at in range(STEPS - 1):
        small[:, :K] = hdot_t(eye, uppers[at][:, :K])
        lows.append(small[...])
    bands = []
    for at in range(STEPS):
        band = pltpu.roll(diags[at], K * at, 1) if at else diags[at]
        if at + 1 < STEPS:
            band = band + pltpu.roll(lows[at], K * (at + 1), 1)
        if at:
            before = uppers[at - 1]
            band = band + (pltpu.roll(before, K * (at - 1), 1) if at > 1 else before)
        bands.append(band)
    bands.append(jnp.zeros((K, LANES), F32))
    krylov = jnp.concatenate(bands, axis=0)
    top = top_value(krylov)
    krylov_ref[...] = krylov / top
    scale_ref[...] = jnp.full(scale_ref.shape, 1.0, F32) / jnp.sqrt(top)

    for step in range(STEPS):
        all_of(tbuf.at[step], t_send.at[step], t_recv.at[step], nt - 1).wait_send()
        if step + 1 < STEPS:
            all_of(fsend.at[step], rs_send.at[step], rs_recv.at[step], nf - 1).wait_send()
            all_of(gathered.at[step], ag_send.at[step], ag_recv.at[step], nf - 1).wait_send()
    all_of(drecv, d_send, d_recv, nf - 1).wait_send()


def lanczos(probes, moment, nf, nt):
    rows, cols = moment.shape
    width = cols // 8
    vmem = pl.BlockSpec(memory_space=pltpu.VMEM)
    dma = pltpu.SemaphoreType.DMA
    return pl.pallas_call(
        functools.partial(lanczos_kernel, nf, nt),
        out_shape=(
            jax.ShapeDtypeStruct((LANES, LANES), F32),
            jax.ShapeDtypeStruct((8, LANES), F32),
        ),
        in_specs=[vmem, vmem],
        out_specs=(vmem, vmem),
        scratch_shapes=[
            pltpu.VMEM((K, cols), F32),
            pltpu.VMEM((STEPS - 1, K, cols), F32),
            pltpu.VMEM((K, LANES), F32),
            pltpu.VMEM((STEPS, nt, K, rows + LANES), F32),
            pltpu.VMEM((STEPS - 1, nf, 8, width + LANES), F32),
            pltpu.VMEM((STEPS - 1, nf, 8, width + LANES), F32),
            pltpu.VMEM((STEPS - 1, nf, 8, width), F32),
            pltpu.VMEM((nf, 8, LANES), F32),
            dma((STEPS,)),
            dma((STEPS,)),
            dma((STEPS - 1,)),
            dma((STEPS - 1,)),
            dma((STEPS - 1,)),
            dma((STEPS - 1,)),
            dma(()),
            dma(()),
        ],
        compiler_params=pltpu.CompilerParams(
            collective_id=0, has_side_effects=True, vmem_limit_bytes=40 * 1024 * 1024
        ),
    )(probes, moment)


def signed(n):
    return (n + 1) % 4 - 1


def mod4(at):
    return at[0] % 4, at[1] % 4


PIECES = (("a", 1), ("a", -1), ("b", 1), ("b", -1))
GROUPS = (
    ((1, 0), (0, 1)),
    ((-1, 0), (0, -1)),
    ((1, 1), (-1, -1)),
    ((1, -1), (-1, 1)),
    ((2, 0), (0, 2)),
    ((2, 1), (1, 2)),
    ((2, -1), (-1, 2)),
    ((2, 2),),
)


def onward(piece, source):
    first, sign = piece
    u, v = signed(-source[0]), signed(-source[1])
    if first == "b":
        u, v = v, u
    out = []
    if v == 0:
        if u == 0:
            out += [(1, 0), (-1, 0)]
        elif u == sign:
            out += [(sign, 0)]
        out += [(0, 1), (0, -1)]
    elif v == sign:
        out += [(0, sign)]
    if first == "b":
        out = [(v, u) for u, v in out]
    return out


def slot(at):
    i, j = mod4(at)
    return 4 * i + j


def gather_kernel(
    nt, tokens_ref, new_ref, out_ref, wall, toks, acc, recv, send, sib_recv, sib_send, tok_sem, out_sem
):
    mf = lax.axis_index("fsdp")
    core = lax.rem(mf, 2)
    chip = lax.div(mf, 2)
    mx, mz = lax.div(chip, 4), lax.rem(chip, 4)
    rows, cols = new_ref.shape
    piece_rows = rows // 4

    def chip_at(at):
        i, j = at
        x = lax.rem(mx + 4 + i * (1 - core) + j * core, 4)
        z = lax.rem(mz + 4 + i * core + j * (1 - core), 4)
        return 4 * x + z

    def device_at(at):
        return {"fsdp": 2 * chip_at(at) + core}

    sibling = {"fsdp": 2 * chip + 1 - core}
    load = pltpu.make_async_copy(tokens_ref, toks, tok_sem)
    load.start()

    barrier = pltpu.get_barrier_semaphore()
    for at in ((1, 0), (-1, 0), (0, 1), (0, -1)):
        pl.semaphore_signal(barrier, inc=1, device_id=device_at(at))
    pl.semaphore_signal(barrier, inc=1, device_id=sibling)
    wall[mf] = new_ref[...]
    pl.semaphore_wait(barrier, 5)

    def part(owner, t):
        return wall.at[owner, pl.ds(t * piece_rows, piece_rows)]

    def start(t, owner, source, to):
        pltpu.make_async_remote_copy(
            src_ref=part(owner, t),
            dst_ref=part(owner, t),
            send_sem=send.at[t],
            recv_sem=recv.at[t, slot((source[0] - to[0], source[1] - to[1]))],
            device_id=device_at(to),
        ).start()

    def to_sibling(t, owner, source):
        pltpu.make_async_remote_copy(
            src_ref=part(owner, t),
            dst_ref=part(owner, t),
            send_sem=sib_send.at[t],
            recv_sem=sib_recv.at[slot((source[1], source[0]))],
            device_id=sibling,
        ).start()

    def arrived(ref, sem):
        return pltpu.make_async_remote_copy(
            src_ref=ref, dst_ref=ref, send_sem=sem, recv_sem=sem, device_id=sibling
        )

    for rank in range(4):
        for t, piece in enumerate(PIECES):
            start(t, mf, (0, 0), onward(piece, (0, 0))[rank])
    for t in range(4):
        to_sibling(t, mf, (0, 0))

    def events(source):
        owner = 2 * chip_at(source) + core
        for t, piece in enumerate(PIECES):
            arrived(part(owner, t), recv.at[t, slot(source)]).wait_recv()
            for to in onward(piece, source):
                start(t, owner, source, to)
            to_sibling(t, owner, source)

    def multiply(source, first=False):
        other = 2 * chip_at(source)
        arrived(wall.at[other + 1 - core], sib_recv.at[slot(source)]).wait_recv()
        left = toks[:, pl.ds(pl.multiple_of(other * rows, 2 * rows), 2 * rows)]

        @pl.loop(0, cols // 512)
        def _(n):
            at = pl.ds(pl.multiple_of(n * 512, 512), 512)
            right = wall[pl.ds(other, 2), :, at].reshape(2 * rows, 512)
            product = jnp.dot(left, right, preferred_element_type=F32)
            if first:
                acc[:, at] = product
            else:
                acc[:, at] += product

    load.wait()
    before = ((0, 0),)
    for group in GROUPS:
        for source in group:
            events(source)
        for source in before:
            multiply(source, first=source == (0, 0))
        before = group
    for source in before:
        multiply(source)
    copy = pltpu.make_async_copy(acc, out_ref, out_sem)
    copy.start()
    for t in range(4):
        sent = wall.at[pl.ds(0, 15), pl.ds(t * piece_rows, piece_rows)]
        arrived(sent, send.at[t]).wait_send()
        sent = wall.at[pl.ds(0, 16), pl.ds(t * piece_rows, piece_rows)]
        arrived(sent, sib_send.at[t]).wait_send()
    copy.wait()


def gather_multiply(tokens, new_weight, nf, nt):
    rows, cols = new_weight.shape
    any_space = pl.BlockSpec(memory_space=pl.ANY)
    dma = pltpu.SemaphoreType.DMA
    count = tokens.shape[0]
    return pl.pallas_call(
        functools.partial(gather_kernel, nt),
        out_shape=jax.ShapeDtypeStruct((count, cols), F32),
        in_specs=[any_space, pl.BlockSpec(memory_space=pltpu.VMEM)],
        out_specs=any_space,
        scratch_shapes=[
            pltpu.VMEM((nf, rows, cols), jnp.bfloat16),
            pltpu.VMEM(tokens.shape, jnp.bfloat16),
            pltpu.VMEM((count, cols), F32),
            dma((4, 16)),
            dma((4,)),
            dma((16,)),
            dma((4,)),
            dma(()),
            dma(()),
        ],
        compiler_params=pltpu.CompilerParams(
            collective_id=1, has_side_effects=True, vmem_limit_bytes=60 * 1024 * 1024
        ),
    )(tokens, new_weight)


def local(nf, nt, tokens, weight, momentum, gradient, probes):
    moment = 0.9 * momentum + gradient.astype(F32)
    krylov, scale = lanczos(probes, moment, nf, nt)
    new_weight = (weight.astype(F32) - moment * scale[0, 0]).astype(jnp.bfloat16)
    summed = gather_multiply(tokens, new_weight, nf, nt)
    size = STEPS * K
    return (summed, moment, krylov[:size, :size])


def solution(mesh):
    return jax.shard_map(
        functools.partial(local, mesh.shape["fsdp"], mesh.shape["tensor"]),
        mesh=mesh,
        in_specs=(
            P("fsdp", None),
            P("fsdp", "tensor"),
            P("fsdp", "tensor"),
            P("fsdp", "tensor"),
            P(None, "tensor"),
        ),
        out_specs=(P("fsdp", "tensor"), P("fsdp", "tensor"), P()),
        check_vma=False,
    )
```

```python
import functools

import jax
import jax.numpy as jnp
from jax import lax
from jax.experimental import pallas as pl
from jax.experimental.pallas import tpu as pltpu
from jax.sharding import PartitionSpec as P

STEPS = 3
K = 32
LANES = 128
HIGHEST = lax.Precision.HIGHEST
F32 = jnp.float32


def hdot(left, right):
    return jnp.dot(left, right, precision=HIGHEST, preferred_element_type=F32)


def hdot_t(left, right):
    return lax.dot_general(
        left, right, (((1,), (1,)), ((), ())), precision=HIGHEST, preferred_element_type=F32
    )


def eliminate(gram):
    lane = lax.broadcasted_iota(jnp.int32, (8, LANES), 1)
    sub = lax.broadcasted_iota(jnp.int32, (8, LANES), 0)
    sub_col = lax.broadcasted_iota(jnp.int32, (8, 1), 0)
    count = K // 8
    blocks = []
    for at in range(count):
        eye = jnp.where(lane == sub + (8 * at + K), 1.0, 0.0)
        blocks.append(gram[8 * at : 8 * at + 8, :] + eye)
    for j in range(K):
        at, row = divmod(j, 8)
        pivot_row = blocks[at][row : row + 1, :]
        inverse = 1.0 / blocks[at][row : row + 1, j : j + 1]
        scaled = pivot_row * inverse
        for other in range(at, count):
            column = blocks[other][:, j : j + 1]
            if other == at:
                column = jnp.where(sub_col > row, column, 0.0)
            blocks[other] = blocks[other] - column * scaled
    upper, inverse_low = [], []
    for at in range(count):
        row = sub + 8 * at
        pivots = jnp.sum(jnp.where(lane == row, blocks[at], 0.0), axis=1, keepdims=True)
        scaled = blocks[at] / jnp.sqrt(pivots)
        upper.append(jnp.where((lane >= row) & (lane < K), scaled, 0.0))
        shifted = pltpu.roll(scaled, LANES - K, 1)
        inverse_low.append(jnp.where(lane <= row, shifted, 0.0))
    return jnp.concatenate(upper, axis=0), jnp.concatenate(inverse_low, axis=0)


def pack(square):
    tile = square[0:8, :]
    for at in range(1, K // 8):
        tile = tile + pltpu.roll(square[8 * at : 8 * at + 8, :], K * at, 1)
    return tile


def unpack(tile):
    lane = lax.broadcasted_iota(jnp.int32, (8, LANES), 1)
    parts = []
    for at in range(K // 8):
        part = tile if at == 0 else pltpu.roll(tile, LANES - K * at, 1)
        parts.append(jnp.where(lane < K, part, 0.0))
    return jnp.concatenate(parts, axis=0)


def top_value(krylov):
    def unit(power):
        return power / jnp.max(jnp.abs(power))

    power = unit(krylov)
    for turn in range(5):
        power = hdot(power, power)
        if turn == 2:
            power = unit(power)
    down = jnp.sum(power, axis=1, keepdims=True)
    along = jnp.sum(power, axis=0, keepdims=True)
    length = jnp.sqrt(jnp.sum(down * down)) * jnp.sqrt(jnp.sum(along * along))
    return jnp.sum(krylov * (down * along)) / length


def signed(n):
    return (n + 1) % 4 - 1


def mod4(at):
    return at[0] % 4, at[1] % 4


PIECES = (("a", 1), ("a", -1), ("b", 1), ("b", -1))
GROUPS = (
    ((1, 0), (0, 1)),
    ((-1, 0), (0, -1)),
    ((1, 1), (-1, -1)),
    ((1, -1), (-1, 1)),
    ((2, 0), (0, 2)),
    ((2, 1), (1, 2)),
    ((2, -1), (-1, 2)),
    ((2, 2),),
)


def onward(piece, source):
    first, sign = piece
    u, v = signed(-source[0]), signed(-source[1])
    if first == "b":
        u, v = v, u
    out = []
    if v == 0:
        if u == 0:
            out += [(1, 0), (-1, 0)]
        elif u == sign:
            out += [(sign, 0)]
        out += [(0, 1), (0, -1)]
    elif v == sign:
        out += [(0, sign)]
    if first == "b":
        out = [(v, u) for u, v in out]
    return out


def slot(at):
    i, j = mod4(at)
    return 4 * i + j


def spans(start, counts):
    out = []
    for count in counts:
        out.append((start, start + count))
        start += count
    return tuple(out)


EARLY = spans(0, (32, 32, 16, 16))
LATE = spans(96, (32, 32, 48, 48))
DURING_TENSOR = ((), (1,), (4,))
DURING_SCATTER = ((), (2,))
DURING_GATHER = ((0,), (3,))
DURING_LAST = (5,)
AFTER = (6, 7)


class Flow:
    def __init__(self, wall, mall, rows, recv, send, sib_recv, sib_send, device_at, sibling):
        self.wall, self.mall, self.rows = wall, mall, rows
        self.recv, self.send, self.sib_recv, self.sib_send = recv, send, sib_recv, sib_send
        self.device_at, self.sibling = device_at, sibling
        self.first, self.last = rows[0][0], rows[-1][1]
        self.kinds = 2 if mall is not None else 1

    def copies(self, owner, low, high, send, recv, to):
        band = pl.ds(low, high - low)
        for ref in (self.wall, self.mall)[: self.kinds]:
            pltpu.make_async_remote_copy(
                src_ref=ref.at[owner, band],
                dst_ref=ref.at[owner, band],
                send_sem=send,
                recv_sem=recv,
                device_id=to,
            ).start()

    def bytes_of(self, count, high_less_low, sem):
        ref = self.wall.at[pl.ds(0, count), pl.ds(0, self.kinds * high_less_low)]
        return pltpu.make_async_remote_copy(
            src_ref=ref, dst_ref=ref, send_sem=sem, recv_sem=sem, device_id=self.sibling
        )

    def pass_on(self, t, owner, source, to):
        low, high = self.rows[t]
        there = self.recv.at[t, slot((source[0] - to[0], source[1] - to[1]))]
        self.copies(owner, low, high, self.send.at[t], there, self.device_at(to))

    def to_sibling(self, owner, source):
        there = self.sib_recv.at[slot((source[1], source[0]))]
        self.copies(owner, self.first, self.last, self.sib_send, there, self.sibling)

    def begin(self, owner):
        for rank in range(4):
            for t, piece in enumerate(PIECES):
                self.pass_on(t, owner, (0, 0), onward(piece, (0, 0))[rank])
        self.to_sibling(owner, (0, 0))

    def events(self, owner, source):
        for t, piece in enumerate(PIECES):
            low, high = self.rows[t]
            self.bytes_of(1, high - low, self.recv.at[t, slot(source)]).wait_recv()
            for to in onward(piece, source):
                self.pass_on(t, owner, source, to)
        self.to_sibling(owner, source)

    def from_sibling(self, owner, source):
        self.bytes_of(1, self.last - self.first, self.sib_recv.at[slot(source)]).wait_recv()

    def sent(self):
        for t, (low, high) in enumerate(self.rows):
            self.bytes_of(15, high - low, self.send.at[t]).wait_send()
        self.bytes_of(16, self.last - self.first, self.sib_send).wait_send()


def step_kernel(
    nf,
    nt,
    tokens_ref,
    weight_ref,
    probes_ref,
    moment_ref,
    out_ref,
    krylov_ref,
    wall,
    mall,
    acc,
    toks,
    block,
    basis,
    small,
    tbuf,
    fsend,
    frecv,
    gathered,
    drecv,
    early_recv,
    early_send,
    early_sib_recv,
    early_sib_send,
    late_recv,
    late_send,
    late_sib_recv,
    late_sib_send,
    tok_sem,
    out_sem,
    t_send,
    t_recv,
    rs_send,
    rs_recv,
    ag_send,
    ag_recv,
    d_send,
    d_recv,
):
    mf = lax.axis_index("fsdp")
    mt = lax.axis_index("tensor")
    rows, cols = moment_ref.shape
    width = cols // 8
    core = lax.rem(mf, 2)
    chip = lax.div(mf, 2)
    mx, mz = lax.div(chip, 4), lax.rem(chip, 4)

    def chip_at(at):
        i, j = at
        x = lax.rem(mx + 4 + i * (1 - core) + j * core, 4)
        z = lax.rem(mz + 4 + i * core + j * (1 - core), 4)
        return 4 * x + z

    def device_at(at):
        return {"fsdp": 2 * chip_at(at) + core}

    sibling = {"fsdp": 2 * chip + 1 - core}

    def fsdp_at(k):
        return {"fsdp": lax.rem(mf + k, nf)}

    def tensor_at(k):
        return {"tensor": lax.rem(mt + k, nt)}

    barrier = pltpu.get_barrier_semaphore()

    @pl.loop(1, nf)
    def _(k):
        pl.semaphore_signal(barrier, inc=1, device_id=fsdp_at(k))

    @pl.loop(1, nt)
    def _(k):
        pl.semaphore_signal(barrier, inc=1, device_id=tensor_at(k))

    lane = lax.broadcasted_iota(jnp.int32, (K, LANES), 1)

    def to_all(src, dst, send, recv):
        @pl.loop(1, nf)
        def _(k):
            pltpu.make_async_remote_copy(
                src_ref=src(lax.rem(mf + k, nf)),
                dst_ref=dst,
                send_sem=send,
                recv_sem=recv,
                device_id=fsdp_at(k),
            ).start()

    def all_of(ref, send, recv, count):
        return pltpu.make_async_remote_copy(
            src_ref=ref.at[pl.ds(0, count)],
            dst_ref=ref.at[pl.ds(0, count)],
            send_sem=send,
            recv_sem=recv,
            device_id=fsdp_at(1),
        )

    early = Flow(wall, mall, EARLY, early_recv, early_send, early_sib_recv, early_sib_send, device_at, sibling)
    late = Flow(wall, None, LATE, late_recv, late_send, late_sib_recv, late_sib_send, device_at, sibling)
    ahead = EARLY[-1][1]

    def owner_at(source):
        return 2 * chip_at(source) + core

    def early_events(*numbers):
        for number in numbers:
            for source in GROUPS[number]:
                early.events(owner_at(source), source)

    wall[mf, :ahead] = weight_ref[:ahead]
    mall[mf] = moment_ref[:ahead].astype(jnp.bfloat16)
    block[...] = probes_ref[...]
    small[...] = jnp.zeros_like(small)
    upper = None
    diags, uppers = [], []
    for step in range(STEPS):
        now = block[...]
        mine = tbuf.at[step, mt]
        mine[:, rows:] = jnp.zeros((K, LANES), F32)
        mine[:, :rows] = hdot_t(now, moment_ref[...])
        mine[:, rows : rows + K] = hdot_t(now, now)
        if step == 0:
            pl.semaphore_wait(barrier, nf + nt - 2)

        @pl.loop(1, nt)
        def _(k):
            pltpu.make_async_remote_copy(
                src_ref=tbuf.at[step, mt],
                dst_ref=tbuf.at[step, mt],
                send_sem=t_send.at[step],
                recv_sem=t_recv.at[step],
                device_id=tensor_at(k),
            ).start()

        if step == 0:
            early.begin(mf)
        early_events(*DURING_TENSOR[step])
        all_of(tbuf.at[step], t_send.at[step], t_recv.at[step], nt - 1).wait_recv()
        total = tbuf[step, 0]
        for other in range(1, nt):
            total = total + tbuf[step, other]
        upper_next, inverse_low = eliminate(total[:, rows:])
        if step:
            uppers.append(upper_next)
        inverse_low = inverse_low[:, :K]
        reduced = hdot(inverse_low, total[:, :rows])
        small[:, :K] = hdot_t(reduced, reduced)
        tile = pack(small[...])
        if step + 1 < STEPS:
            images = hdot(reduced, moment_ref[...])
            for r in range(4):
                for c in range(8):
                    fsend[step, 8 * r + c, :, :width] = images[
                        8 * r : 8 * r + 8, width * c : width * (c + 1)
                    ]
                    fsend[step, 8 * r + c, :, width:] = tile
            frecv[step, mf] = fsend[step, mf]
            to_all(
                lambda dest: fsend.at[step, dest],
                frecv.at[step, mf],
                rs_send.at[step],
                rs_recv.at[step],
            )
            basis[step] = hdot(inverse_low, now)
            early_events(*DURING_SCATTER[step])
            all_of(frecv.at[step], rs_send.at[step], rs_recv.at[step], nf - 1).wait_recv()
            summed = jnp.sum(frecv[step], axis=0)
            gathered[step, mf] = summed[:, :width]
            to_all(
                lambda dest: gathered.at[step, mf],
                gathered.at[step, mf],
                ag_send.at[step],
                ag_recv.at[step],
            )
            diag = unpack(summed[:, width:])
            rest = hdot(diag[:, :K], basis[step])
            if step:
                rest = rest + hdot(upper_next[:, :K], basis[step - 1])
            block[...] = rest
            early_events(*DURING_GATHER[step])
            all_of(gathered.at[step], ag_send.at[step], ag_recv.at[step], nf - 1).wait_recv()
            for r in range(4):
                for c in range(8):
                    where = (slice(8 * r, 8 * r + 8), slice(width * c, width * (c + 1)))
                    block[where] = gathered[step, 8 * r + c] - block[where]
        else:
            drecv[mf] = tile
            to_all(lambda dest: drecv.at[mf], drecv.at[mf], d_send, d_recv)
            early_events(*DURING_LAST)
            all_of(drecv, d_send, d_recv, nf - 1).wait_recv()
            diag = unpack(jnp.sum(drecv[...], axis=0))
        diags.append(diag)

    eye = jnp.where(lax.broadcasted_iota(jnp.int32, (K, K), 0) == lax.broadcasted_iota(jnp.int32, (K, K), 1), 1.0, 0.0)
    lows = []
    for at in range(STEPS - 1):
        small[:, :K] = hdot_t(eye, uppers[at][:, :K])
        lows.append(small[...])
    bands = []
    for at in range(STEPS):
        band = pltpu.roll(diags[at], K * at, 1) if at else diags[at]
        if at + 1 < STEPS:
            band = band + pltpu.roll(lows[at], K * (at + 1), 1)
        if at:
            before = uppers[at - 1]
            band = band + (pltpu.roll(before, K * (at - 1), 1) if at > 1 else before)
        bands.append(band)
    bands.append(jnp.zeros((K, LANES), F32))
    krylov = jnp.concatenate(bands, axis=0)
    top = top_value(krylov)
    krylov_ref[...] = krylov / top
    scale = 1.0 / jnp.sqrt(top)
    fresh = weight_ref[ahead:].astype(F32) - moment_ref[ahead:] * scale
    wall[mf, ahead:] = fresh.astype(jnp.bfloat16)
    late.begin(mf)

    early_events(*AFTER)
    early.sent()

    order = [(0, 0)] + [source for group in GROUPS for source in group]

    def tokens_of(number):
        columns = pl.ds(pl.multiple_of(chip_at(order[number]) * 2 * rows, 2 * rows), 2 * rows)
        return pltpu.make_async_copy(
            tokens_ref.at[:, columns], toks.at[number % 2], tok_sem.at[number % 2]
        )

    tokens_of(0).start()

    def multiply(source):
        number = order.index(source)
        if number + 1 < len(order):
            tokens_of(number + 1).start()
        left_owner = 2 * chip_at(source)
        early.from_sibling(left_owner + 1 - core, source)
        for at in range(2):

            @pl.loop(0, ahead // 16)
            def _(n):
                band = pl.ds(pl.multiple_of(n * 16, 16), 16)
                value = wall[left_owner + at, band].astype(F32)
                value = value - mall[left_owner + at, band].astype(F32) * scale
                wall[left_owner + at, band] = value.astype(jnp.bfloat16)

        late.from_sibling(left_owner + 1 - core, source)
        tokens_of(number).wait()
        left = toks[number % 2]

        @pl.loop(0, cols // 512)
        def _(n):
            at = pl.ds(pl.multiple_of(n * 512, 512), 512)
            right = wall[pl.ds(left_owner, 2), :, at].reshape(2 * rows, 512)
            product = jnp.dot(left, right, preferred_element_type=F32)
            if number:
                acc[:, at] += product
            else:
                acc[:, at] = product

    before = ((0, 0),)
    for group in GROUPS:
        for source in group:
            late.events(owner_at(source), source)
        for source in before:
            multiply(source)
        before = group
    for source in before:
        multiply(source)
    copy = pltpu.make_async_copy(acc, out_ref, out_sem)
    copy.start()
    late.sent()
    for step in range(STEPS):
        all_of(tbuf.at[step], t_send.at[step], t_recv.at[step], nt - 1).wait_send()
        if step + 1 < STEPS:
            all_of(fsend.at[step], rs_send.at[step], rs_recv.at[step], nf - 1).wait_send()
            all_of(gathered.at[step], ag_send.at[step], ag_recv.at[step], nf - 1).wait_send()
    all_of(drecv, d_send, d_recv, nf - 1).wait_send()
    copy.wait()


def step_call(tokens, weight, probes, moment, nf, nt):
    rows, cols = moment.shape
    width = cols // 8
    count = tokens.shape[0]
    vmem = pl.BlockSpec(memory_space=pltpu.VMEM)
    anywhere = pl.BlockSpec(memory_space=pl.ANY)
    dma = pltpu.SemaphoreType.DMA
    return pl.pallas_call(
        functools.partial(step_kernel, nf, nt),
        out_shape=(
            jax.ShapeDtypeStruct((count, cols), F32),
            jax.ShapeDtypeStruct((LANES, LANES), F32),
        ),
        in_specs=[anywhere, vmem, vmem, vmem],
        out_specs=(anywhere, vmem),
        scratch_shapes=[
            pltpu.VMEM((nf, rows, cols), jnp.bfloat16),
            pltpu.VMEM((nf, EARLY[-1][1], cols), jnp.bfloat16),
            pltpu.VMEM((count, cols), F32),
            pltpu.VMEM((2, count, 2 * rows), jnp.bfloat16),
            pltpu.VMEM((K, cols), F32),
            pltpu.VMEM((STEPS - 1, K, cols), F32),
            pltpu.VMEM((K, LANES), F32),
            pltpu.VMEM((STEPS, nt, K, rows + LANES), F32),
            pltpu.VMEM((STEPS - 1, nf, 8, width + LANES), F32),
            pltpu.VMEM((STEPS - 1, nf, 8, width + LANES), F32),
            pltpu.VMEM((STEPS - 1, nf, 8, width), F32),
            pltpu.VMEM((nf, 8, LANES), F32),
            dma((4, 16)),
            dma((4,)),
            dma((16,)),
            dma(()),
            dma((4, 16)),
            dma((4,)),
            dma((16,)),
            dma(()),
            dma((2,)),
            dma(()),
            dma((STEPS,)),
            dma((STEPS,)),
            dma((STEPS - 1,)),
            dma((STEPS - 1,)),
            dma((STEPS - 1,)),
            dma((STEPS - 1,)),
            dma(()),
            dma(()),
        ],
        compiler_params=pltpu.CompilerParams(
            collective_id=0, has_side_effects=True, vmem_limit_bytes=62 * 1024 * 1024
        ),
    )(tokens, weight, probes, moment)


def local(nf, nt, tokens, weight, momentum, gradient, probes):
    moment = 0.9 * momentum + gradient.astype(F32)
    summed, krylov = step_call(tokens, weight, probes, moment, nf, nt)
    size = STEPS * K
    return (summed, moment, krylov[:size, :size])


def solution(mesh):
    return jax.shard_map(
        functools.partial(local, mesh.shape["fsdp"], mesh.shape["tensor"]),
        mesh=mesh,
        in_specs=(
            P("fsdp", None),
            P("fsdp", "tensor"),
            P("fsdp", "tensor"),
            P("fsdp", "tensor"),
            P(None, "tensor"),
        ),
        out_specs=(P("fsdp", "tensor"), P("fsdp", "tensor"), P()),
        check_vma=False,
    )
```

```python
import functools

import jax
import jax.numpy as jnp
from jax import lax
from jax.experimental import pallas as pl
from jax.experimental.pallas import tpu as pltpu
from jax.sharding import PartitionSpec as P

STEPS = 3
K = 32
LANES = 128
HIGHEST = lax.Precision.HIGHEST
F32 = jnp.float32


def hdot(left, right):
    return jnp.dot(left, right, precision=HIGHEST, preferred_element_type=F32)


def hdot_t(left, right):
    return lax.dot_general(
        left, right, (((1,), (1,)), ((), ())), precision=HIGHEST, preferred_element_type=F32
    )


def split(value):
    high = value.astype(jnp.bfloat16)
    rest = value - high.astype(F32)
    middle = rest.astype(jnp.bfloat16)
    return high, middle, (rest - middle.astype(F32)).astype(jnp.bfloat16)


def split_dot(left, right, contract):
    def dot(a, b):
        return lax.dot_general(a, b, (((1,), (contract,)), ((), ())), preferred_element_type=F32)

    high, middle, low = split(left)
    first = dot(jnp.concatenate([high, middle, low], axis=0), right[0])
    second = dot(jnp.concatenate([high, middle], axis=0), right[1])
    third = dot(high, right[2])
    small = first[2 * K :] + second[K:] + third
    return first[:K] + ((first[K : 2 * K] + second[:K]) + small)


def eliminate(gram):
    lane = lax.broadcasted_iota(jnp.int32, (8, LANES), 1)
    sub = lax.broadcasted_iota(jnp.int32, (8, LANES), 0)
    sub_col = lax.broadcasted_iota(jnp.int32, (8, 1), 0)
    count = K // 8
    blocks = []
    for at in range(count):
        eye = jnp.where(lane == sub + (8 * at + K), 1.0, 0.0)
        blocks.append(gram[8 * at : 8 * at + 8, :] + eye)
    for j in range(K):
        at, row = divmod(j, 8)
        pivot_row = blocks[at][row : row + 1, :]
        inverse = 1.0 / blocks[at][row : row + 1, j : j + 1]
        scaled = pivot_row * inverse
        for other in range(at, count):
            column = blocks[other][:, j : j + 1]
            if other == at:
                column = jnp.where(sub_col > row, column, 0.0)
            blocks[other] = blocks[other] - column * scaled
    upper, inverse_low = [], []
    for at in range(count):
        row = sub + 8 * at
        pivots = jnp.sum(jnp.where(lane == row, blocks[at], 0.0), axis=1, keepdims=True)
        scaled = blocks[at] / jnp.sqrt(pivots)
        upper.append(jnp.where((lane >= row) & (lane < K), scaled, 0.0))
        shifted = pltpu.roll(scaled, LANES - K, 1)
        inverse_low.append(jnp.where(lane <= row, shifted, 0.0))
    return jnp.concatenate(upper, axis=0), jnp.concatenate(inverse_low, axis=0)


def pack(square):
    tile = square[0:8, :]
    for at in range(1, K // 8):
        tile = tile + pltpu.roll(square[8 * at : 8 * at + 8, :], K * at, 1)
    return tile


def unpack(tile):
    lane = lax.broadcasted_iota(jnp.int32, (8, LANES), 1)
    parts = []
    for at in range(K // 8):
        part = tile if at == 0 else pltpu.roll(tile, LANES - K * at, 1)
        parts.append(jnp.where(lane < K, part, 0.0))
    return jnp.concatenate(parts, axis=0)


def top_value(krylov):
    def unit(power):
        return power / jnp.max(jnp.abs(power))

    power = unit(krylov)
    for turn in range(5):
        power = hdot(power, power)
        if turn == 2:
            power = unit(power)
    down = jnp.sum(power, axis=1, keepdims=True)
    along = jnp.sum(power, axis=0, keepdims=True)
    length = jnp.sqrt(jnp.sum(down * down)) * jnp.sqrt(jnp.sum(along * along))
    return jnp.sum(krylov * (down * along)) / length


def signed(n):
    return (n + 1) % 4 - 1


def mod4(at):
    return at[0] % 4, at[1] % 4


PIECES = (("a", 1), ("a", -1), ("b", 1), ("b", -1))
GROUPS = (
    ((1, 0), (0, 1)),
    ((-1, 0), (0, -1)),
    ((1, 1), (-1, -1)),
    ((1, -1), (-1, 1)),
    ((2, 0), (0, 2)),
    ((2, 1), (1, 2)),
    ((2, -1), (-1, 2)),
    ((2, 2),),
)


def onward(piece, source):
    first, sign = piece
    u, v = signed(-source[0]), signed(-source[1])
    if first == "b":
        u, v = v, u
    out = []
    if v == 0:
        if u == 0:
            out += [(1, 0), (-1, 0)]
        elif u == sign:
            out += [(sign, 0)]
        out += [(0, 1), (0, -1)]
    elif v == sign:
        out += [(0, sign)]
    if first == "b":
        out = [(v, u) for u, v in out]
    return out


def slot(at):
    i, j = mod4(at)
    return 4 * i + j


def spans(start, counts):
    out = []
    for count in counts:
        out.append((start, start + count))
        start += count
    return tuple(out)


EARLY = spans(0, (16, 16, 16, 16))
LATE = spans(64, (48, 48, 48, 48))
DURING_TENSOR = ((), (0, 1), (2, 3, 4))
AFTER = (5, 6, 7)


class Flow:
    def __init__(self, wall, mall, rows, recv, send, sib_recv, sib_send, device_at, sibling):
        self.wall, self.mall, self.rows = wall, mall, rows
        self.recv, self.send, self.sib_recv, self.sib_send = recv, send, sib_recv, sib_send
        self.device_at, self.sibling = device_at, sibling
        self.first, self.last = rows[0][0], rows[-1][1]
        self.kinds = 2 if mall is not None else 1

    def copies(self, owner, low, high, send, recv, to):
        band = pl.ds(low, high - low)
        for ref in (self.wall, self.mall)[: self.kinds]:
            pltpu.make_async_remote_copy(
                src_ref=ref.at[owner, band],
                dst_ref=ref.at[owner, band],
                send_sem=send,
                recv_sem=recv,
                device_id=to,
            ).start()

    def bytes_of(self, count, high_less_low, sem):
        ref = self.wall.at[pl.ds(0, count), pl.ds(0, self.kinds * high_less_low)]
        return pltpu.make_async_remote_copy(
            src_ref=ref, dst_ref=ref, send_sem=sem, recv_sem=sem, device_id=self.sibling
        )

    def pass_on(self, t, owner, source, to):
        low, high = self.rows[t]
        there = self.recv.at[t, slot((source[0] - to[0], source[1] - to[1]))]
        self.copies(owner, low, high, self.send.at[t], there, self.device_at(to))

    def to_sibling(self, owner, source):
        there = self.sib_recv.at[slot((source[1], source[0]))]
        self.copies(owner, self.first, self.last, self.sib_send, there, self.sibling)

    def begin(self, owner):
        for rank in range(4):
            for t, piece in enumerate(PIECES):
                self.pass_on(t, owner, (0, 0), onward(piece, (0, 0))[rank])
        self.to_sibling(owner, (0, 0))

    def events(self, owner, source):
        for t, piece in enumerate(PIECES):
            low, high = self.rows[t]
            self.bytes_of(1, high - low, self.recv.at[t, slot(source)]).wait_recv()
            for to in onward(piece, source):
                self.pass_on(t, owner, source, to)
        self.to_sibling(owner, source)

    def from_sibling(self, owner, source):
        self.bytes_of(1, self.last - self.first, self.sib_recv.at[slot(source)]).wait_recv()

    def sent(self):
        for t, (low, high) in enumerate(self.rows):
            self.bytes_of(15, high - low, self.send.at[t]).wait_send()
        self.bytes_of(16, self.last - self.first, self.sib_send).wait_send()


def step_kernel(
    nf,
    nt,
    tokens_ref,
    weight_ref,
    probes_ref,
    momentum_ref,
    gradient_ref,
    partial_ref,
    last_ref,
    krylov_ref,
    wall,
    mall,
    acc,
    toks,
    block,
    basis,
    small,
    parts,
    gbuf,
    tbuf,
    fsend,
    frecv,
    gathered,
    drecv,
    early_recv,
    early_send,
    early_sib_recv,
    early_sib_send,
    late_recv,
    late_send,
    late_sib_recv,
    late_sib_send,
    tok_sem,
    out_sem,
    g_send,
    g_recv,
    t_send,
    t_recv,
    rs_send,
    rs_recv,
    ag_send,
    ag_recv,
    d_send,
    d_recv,
):
    mf = lax.axis_index("fsdp")
    mt = lax.axis_index("tensor")
    rows, cols = momentum_ref.shape
    width = cols // 8
    core = lax.rem(mf, 2)
    chip = lax.div(mf, 2)
    mx, mz = lax.div(chip, 4), lax.rem(chip, 4)

    def chip_at(at):
        i, j = at
        x = lax.rem(mx + 4 + i * (1 - core) + j * core, 4)
        z = lax.rem(mz + 4 + i * core + j * (1 - core), 4)
        return 4 * x + z

    def device_at(at):
        return {"fsdp": 2 * chip_at(at) + core}

    sibling = {"fsdp": 2 * chip + 1 - core}

    def fsdp_at(k):
        return {"fsdp": lax.rem(mf + k, nf)}

    def tensor_at(k):
        return {"tensor": lax.rem(mt + k, nt)}

    barrier = pltpu.get_barrier_semaphore()

    @pl.loop(1, nf)
    def _(k):
        pl.semaphore_signal(barrier, inc=1, device_id=fsdp_at(k))

    @pl.loop(1, nt)
    def _(k):
        pl.semaphore_signal(barrier, inc=1, device_id=tensor_at(k))

    lane = lax.broadcasted_iota(jnp.int32, (K, LANES), 1)

    def to_all(src, dst, send, recv):
        @pl.loop(1, nf)
        def _(k):
            pltpu.make_async_remote_copy(
                src_ref=src(lax.rem(mf + k, nf)),
                dst_ref=dst,
                send_sem=send,
                recv_sem=recv,
                device_id=fsdp_at(k),
            ).start()

    def to_tensor(ref, send, recv):
        for k in range(1, nt):
            pltpu.make_async_remote_copy(
                src_ref=ref,
                dst_ref=ref,
                send_sem=send,
                recv_sem=recv,
                device_id=tensor_at(k),
            ).start()

    def all_of(ref, send, recv, count):
        return pltpu.make_async_remote_copy(
            src_ref=ref.at[pl.ds(0, count)],
            dst_ref=ref.at[pl.ds(0, count)],
            send_sem=send,
            recv_sem=recv,
            device_id=fsdp_at(1),
        )

    early = Flow(wall, mall, EARLY, early_recv, early_send, early_sib_recv, early_sib_send, device_at, sibling)
    late = Flow(wall, None, LATE, late_recv, late_send, late_sib_recv, late_sib_send, device_at, sibling)
    ahead = EARLY[-1][1]

    def owner_at(source):
        return 2 * chip_at(source) + core

    def early_events(*numbers):
        for number in numbers:
            for source in GROUPS[number]:
                early.events(owner_at(source), source)

    block[...] = probes_ref[...]
    small[...] = jnp.zeros_like(small)

    def send_gram(step, now):
        small[:, :K] = hdot_t(now, now)
        gbuf[step, mt] = pack(small[...])
        if step == 0:
            pl.semaphore_wait(barrier, nf + nt - 2)
        to_tensor(gbuf.at[step, mt], g_send.at[step], g_recv.at[step])

    send_gram(0, probes_ref[...])
    moment = 0.9 * momentum_ref[...] + gradient_ref[...].astype(F32)
    for at, value in enumerate(split(moment)):
        parts[at] = value
    wall[mf, :ahead] = weight_ref[:ahead]
    mall[mf] = parts[0, :ahead]
    diags, uppers = [], []
    for step in range(STEPS):
        now = block[...]
        if step:
            send_gram(step, now)
        tbuf[step, mt] = split_dot(now, parts, 1)
        to_tensor(tbuf.at[step, mt], t_send.at[step], t_recv.at[step])
        if step == 0:
            early.begin(mf)
        all_of(gbuf.at[step], g_send.at[step], g_recv.at[step], nt - 1).wait_recv()
        gram = gbuf[step, 0]
        for other in range(1, nt):
            gram = gram + gbuf[step, other]
        upper_next, inverse_low = eliminate(unpack(gram))
        if step:
            uppers.append(upper_next)
        early_events(*DURING_TENSOR[step])
        all_of(tbuf.at[step], t_send.at[step], t_recv.at[step], nt - 1).wait_recv()
        total = tbuf[step, 0]
        for other in range(1, nt):
            total = total + tbuf[step, other]
        inverse_low = inverse_low[:, :K]
        reduced = hdot(inverse_low, total)
        small[:, :K] = hdot_t(reduced, reduced)
        tile = pack(small[...])
        if step + 1 < STEPS:
            drecv[step, mf] = tile
            images = split_dot(reduced, parts, 0)
            for r in range(4):
                for c in range(8):
                    fsend[step, 8 * r + c] = images[
                        8 * r : 8 * r + 8, width * c : width * (c + 1)
                    ]
            frecv[step, mf] = fsend[step, mf]
            to_all(
                lambda dest: fsend.at[step, dest],
                frecv.at[step, mf],
                rs_send.at[step],
                rs_recv.at[step],
            )
            to_all(
                lambda dest: drecv.at[step, mf], drecv.at[step, mf], d_send.at[step], d_recv.at[step]
            )
            basis[step] = hdot(inverse_low, now)
            all_of(frecv.at[step], rs_send.at[step], rs_recv.at[step], nf - 1).wait_recv()
            summed = jnp.sum(frecv[step], axis=0)
            gathered[step, mf] = summed
            to_all(
                lambda dest: gathered.at[step, mf],
                gathered.at[step, mf],
                ag_send.at[step],
                ag_recv.at[step],
            )
            all_of(drecv.at[step], d_send.at[step], d_recv.at[step], nf - 1).wait_recv()
            diag = unpack(jnp.sum(drecv[step], axis=0))
            rest = hdot(diag[:, :K], basis[step])
            if step:
                rest = rest + hdot(upper_next[:, :K], basis[step - 1])
            block[...] = rest
            all_of(gathered.at[step], ag_send.at[step], ag_recv.at[step], nf - 1).wait_recv()
            for r in range(4):
                for c in range(8):
                    where = (slice(8 * r, 8 * r + 8), slice(width * c, width * (c + 1)))
                    block[where] = gathered[step, 8 * r + c] - block[where]
        else:
            drecv[step, mf] = tile
            to_all(
                lambda dest: drecv.at[step, mf], drecv.at[step, mf], d_send.at[step], d_recv.at[step]
            )
            all_of(drecv.at[step], d_send.at[step], d_recv.at[step], nf - 1).wait_recv()
            diag = unpack(jnp.sum(drecv[step], axis=0))
        diags.append(diag)

    eye = jnp.where(lax.broadcasted_iota(jnp.int32, (K, K), 0) == lax.broadcasted_iota(jnp.int32, (K, K), 1), 1.0, 0.0)
    lows = []
    for at in range(STEPS - 1):
        small[:, :K] = hdot_t(eye, uppers[at][:, :K])
        lows.append(small[...])
    bands = []
    for at in range(STEPS):
        band = pltpu.roll(diags[at], K * at, 1) if at else diags[at]
        if at + 1 < STEPS:
            band = band + pltpu.roll(lows[at], K * (at + 1), 1)
        if at:
            before = uppers[at - 1]
            band = band + (pltpu.roll(before, K * (at - 1), 1) if at > 1 else before)
        bands.append(band)
    bands.append(jnp.zeros((K, LANES), F32))
    krylov = jnp.concatenate(bands, axis=0)
    top = top_value(krylov)
    krylov_ref[...] = krylov / top
    scale = 1.0 / jnp.sqrt(top)
    fresh = 0.9 * momentum_ref[ahead:] + gradient_ref[ahead:].astype(F32)
    fresh = weight_ref[ahead:].astype(F32) - fresh * scale
    wall[mf, ahead:] = fresh.astype(jnp.bfloat16)
    late.begin(mf)

    early_events(*AFTER)
    early.sent()

    order = [(0, 0)] + [source for group in GROUPS for source in group]

    def tokens_of(number):
        columns = pl.ds(pl.multiple_of(chip_at(order[number]) * 2 * rows, 2 * rows), 2 * rows)
        return pltpu.make_async_copy(
            tokens_ref.at[:, columns], toks.at[number % 2], tok_sem.at[number % 2]
        )

    tokens_of(0).start()

    def combine(source):
        owner = 2 * chip_at(source)
        early.from_sibling(owner + 1 - core, source)
        for at in range(2):

            @pl.loop(0, ahead // 16)
            def _(n):
                band = pl.ds(pl.multiple_of(n * 16, 16), 16)
                value = wall[owner + at, band].astype(F32)
                value = value - mall[owner + at, band].astype(F32) * scale
                wall[owner + at, band] = value.astype(jnp.bfloat16)

    def multiply(source):
        number = order.index(source)
        if number + 2 < len(order):
            tokens_of(number + 1).start()
        left_owner = 2 * chip_at(source)
        combine(source)
        late.from_sibling(left_owner + 1 - core, source)
        tokens_of(number).wait()
        left = toks[number % 2]

        @pl.loop(0, cols // 512)
        def _(n):
            at = pl.ds(pl.multiple_of(n * 512, 512), 512)
            right = wall[pl.ds(left_owner, 2), :, at].reshape(2 * rows, 512)
            product = jnp.dot(left, right, preferred_element_type=F32)
            if number:
                acc[:, at] += product
            else:
                acc[:, at] = product

    before = ((0, 0),)
    for group in GROUPS[:-1]:
        for source in group:
            late.events(owner_at(source), source)
        for source in before:
            multiply(source)
        before = group
    for source in before:
        multiply(source)
    partial = pltpu.make_async_copy(acc, partial_ref, out_sem)
    partial.start()
    last = GROUPS[-1][0]
    combine(last)
    late.events(owner_at(last), last)
    late.from_sibling(2 * chip_at(last) + 1 - core, last)
    final = pltpu.make_async_copy(wall.at[pl.ds(2 * chip_at(last), 2)], last_ref, tok_sem.at[0])
    final.start()
    late.sent()
    for step in range(STEPS):
        all_of(gbuf.at[step], g_send.at[step], g_recv.at[step], nt - 1).wait_send()
        all_of(tbuf.at[step], t_send.at[step], t_recv.at[step], nt - 1).wait_send()
        all_of(drecv.at[step], d_send.at[step], d_recv.at[step], nf - 1).wait_send()
        if step + 1 < STEPS:
            all_of(fsend.at[step], rs_send.at[step], rs_recv.at[step], nf - 1).wait_send()
            all_of(gathered.at[step], ag_send.at[step], ag_recv.at[step], nf - 1).wait_send()
    partial.wait()
    final.wait()


def step_call(tokens, weight, momentum, gradient, probes, nf, nt):
    rows, cols = momentum.shape
    width = cols // 8
    count = tokens.shape[0]
    vmem = pl.BlockSpec(memory_space=pltpu.VMEM)
    anywhere = pl.BlockSpec(memory_space=pl.ANY)
    dma = pltpu.SemaphoreType.DMA
    return pl.pallas_call(
        functools.partial(step_kernel, nf, nt),
        out_shape=(
            jax.ShapeDtypeStruct((count, cols), F32),
            jax.ShapeDtypeStruct((2, rows, cols), jnp.bfloat16),
            jax.ShapeDtypeStruct((LANES, LANES), F32),
        ),
        in_specs=[anywhere, vmem, vmem, vmem, vmem],
        out_specs=(anywhere, anywhere, vmem),
        scratch_shapes=[
            pltpu.VMEM((nf, rows, cols), jnp.bfloat16),
            pltpu.VMEM((nf, EARLY[-1][1], cols), jnp.bfloat16),
            pltpu.VMEM((count, cols), F32),
            pltpu.VMEM((2, count, 2 * rows), jnp.bfloat16),
            pltpu.VMEM((K, cols), F32),
            pltpu.VMEM((STEPS - 1, K, cols), F32),
            pltpu.VMEM((K, LANES), F32),
            pltpu.VMEM((3, rows, cols), jnp.bfloat16),
            pltpu.VMEM((STEPS, nt, 8, LANES), F32),
            pltpu.VMEM((STEPS, nt, K, rows), F32),
            pltpu.VMEM((STEPS - 1, nf, 8, width), F32),
            pltpu.VMEM((STEPS - 1, nf, 8, width), F32),
            pltpu.VMEM((STEPS - 1, nf, 8, width), F32),
            pltpu.VMEM((STEPS, nf, 8, LANES), F32),
            dma((4, 16)),
            dma((4,)),
            dma((16,)),
            dma(()),
            dma((4, 16)),
            dma((4,)),
            dma((16,)),
            dma(()),
            dma((2,)),
            dma(()),
            dma((STEPS,)),
            dma((STEPS,)),
            dma((STEPS,)),
            dma((STEPS,)),
            dma((STEPS - 1,)),
            dma((STEPS - 1,)),
            dma((STEPS - 1,)),
            dma((STEPS - 1,)),
            dma((STEPS,)),
            dma((STEPS,)),
        ],
        compiler_params=pltpu.CompilerParams(
            collective_id=0, has_side_effects=True, vmem_limit_bytes=63 * 1024 * 1024
        ),
    )(tokens, weight, probes, momentum, gradient)


def finish_kernel(
    chip_ref,
    partial_ref,
    tokens_ref,
    last_ref,
    momentum_ref,
    gradient_ref,
    krylov_ref,
    out_ref,
    moment_ref,
    scaled_ref,
):
    both, rows, cols = last_ref.shape
    right = last_ref[...].reshape(both * rows, cols)
    out_ref[...] = partial_ref[...] + jnp.dot(tokens_ref[...], right, preferred_element_type=F32)
    moment_ref[...] = 0.9 * momentum_ref[...] + gradient_ref[...].astype(F32)
    size = scaled_ref.shape[0]
    scaled_ref[...] = krylov_ref[:size, :size]


def finish(chip, partial, tokens, last, momentum, gradient, krylov):
    count, cols = partial.shape
    rows = momentum.shape[0]
    turns = 8
    size = STEPS * K
    by_cols = pl.BlockSpec((count, cols // turns), lambda n, chip: (0, n))
    by_rows = pl.BlockSpec((rows // turns, cols), lambda n, chip: (n, 0))
    return pl.pallas_call(
        finish_kernel,
        grid_spec=pltpu.PrefetchScalarGridSpec(
            num_scalar_prefetch=1,
            grid=(turns,),
            in_specs=[
                by_cols,
                pl.BlockSpec((count, 2 * rows), lambda n, chip: (0, chip[0])),
                pl.BlockSpec((2, rows, cols // turns), lambda n, chip: (0, 0, n)),
                by_rows,
                by_rows,
                pl.BlockSpec((LANES, LANES), lambda n, chip: (0, 0)),
            ],
            out_specs=(by_cols, by_rows, pl.BlockSpec((size, size), lambda n, chip: (0, 0))),
        ),
        out_shape=(
            jax.ShapeDtypeStruct((count, cols), F32),
            jax.ShapeDtypeStruct((rows, cols), F32),
            jax.ShapeDtypeStruct((size, size), F32),
        ),
    )(chip, partial, tokens, last, momentum, gradient, krylov)


def local(nf, nt, tokens, weight, momentum, gradient, probes):
    partial, last, krylov = step_call(tokens, weight, momentum, gradient, probes, nf, nt)
    chip = lax.div(lax.axis_index("fsdp"), 2)
    far = 4 * lax.rem(lax.div(chip, 4) + 2, 4) + lax.rem(chip + 2, 4)
    return finish(far.reshape(1), partial, tokens, last, momentum, gradient, krylov)


def solution(mesh):
    return jax.shard_map(
        functools.partial(local, mesh.shape["fsdp"], mesh.shape["tensor"]),
        mesh=mesh,
        in_specs=(
            P("fsdp", None),
            P("fsdp", "tensor"),
            P("fsdp", "tensor"),
            P("fsdp", "tensor"),
            P(None, "tensor"),
        ),
        out_specs=(P("fsdp", "tensor"), P("fsdp", "tensor"), P()),
        check_vma=False,
    )
```

```python
import functools

import jax
import jax.numpy as jnp
from jax import lax
from jax.experimental import pallas as pl
from jax.experimental.pallas import tpu as pltpu
from jax.sharding import PartitionSpec as P

STEPS = 3
K = 32
LANES = 128
HIGHEST = lax.Precision.HIGHEST
F32 = jnp.float32


def hdot(left, right):
    return jnp.dot(left, right, precision=HIGHEST, preferred_element_type=F32)


def hdot_t(left, right):
    return lax.dot_general(
        left, right, (((1,), (1,)), ((), ())), precision=HIGHEST, preferred_element_type=F32
    )


def split(value):
    high = value.astype(jnp.bfloat16)
    rest = value - high.astype(F32)
    middle = rest.astype(jnp.bfloat16)
    return high, middle, (rest - middle.astype(F32)).astype(jnp.bfloat16)


def split_dot(left, right, contract):
    def dot(a, b):
        return lax.dot_general(a, b, (((1,), (contract,)), ((), ())), preferred_element_type=F32)

    high, middle, low = split(left)
    first = dot(jnp.concatenate([high, middle, low], axis=0), right[0])
    second = dot(jnp.concatenate([high, middle], axis=0), right[1])
    third = dot(high, right[2])
    small = first[2 * K :] + second[K:] + third
    return first[:K] + ((first[K : 2 * K] + second[:K]) + small)


def eliminate(gram):
    lane = lax.broadcasted_iota(jnp.int32, (8, LANES), 1)
    sub = lax.broadcasted_iota(jnp.int32, (8, LANES), 0)
    sub_col = lax.broadcasted_iota(jnp.int32, (8, 1), 0)
    count = K // 8
    blocks = []
    for at in range(count):
        eye = jnp.where(lane == sub + (8 * at + K), 1.0, 0.0)
        blocks.append(gram[8 * at : 8 * at + 8, :] + eye)
    for j in range(K):
        at, row = divmod(j, 8)
        pivot_row = blocks[at][row : row + 1, :]
        inverse = 1.0 / blocks[at][row : row + 1, j : j + 1]
        scaled = pivot_row * inverse
        for other in range(at, count):
            column = blocks[other][:, j : j + 1]
            if other == at:
                column = jnp.where(sub_col > row, column, 0.0)
            blocks[other] = blocks[other] - column * scaled
    upper, inverse_low = [], []
    for at in range(count):
        row = sub + 8 * at
        pivots = jnp.sum(jnp.where(lane == row, blocks[at], 0.0), axis=1, keepdims=True)
        scaled = blocks[at] / jnp.sqrt(pivots)
        upper.append(jnp.where((lane >= row) & (lane < K), scaled, 0.0))
        shifted = pltpu.roll(scaled, LANES - K, 1)
        inverse_low.append(jnp.where(lane <= row, shifted, 0.0))
    return jnp.concatenate(upper, axis=0), jnp.concatenate(inverse_low, axis=0)


def pack(square):
    tile = square[0:8, :]
    for at in range(1, K // 8):
        tile = tile + pltpu.roll(square[8 * at : 8 * at + 8, :], K * at, 1)
    return tile


def unpack(tile):
    lane = lax.broadcasted_iota(jnp.int32, (8, LANES), 1)
    parts = []
    for at in range(K // 8):
        part = tile if at == 0 else pltpu.roll(tile, LANES - K * at, 1)
        parts.append(jnp.where(lane < K, part, 0.0))
    return jnp.concatenate(parts, axis=0)


def top_value(krylov):
    def unit(power):
        return power / jnp.max(jnp.abs(power))

    power = unit(krylov)
    for turn in range(5):
        power = hdot(power, power)
        if turn == 2:
            power = unit(power)
    down = jnp.sum(power, axis=1, keepdims=True)
    along = jnp.sum(power, axis=0, keepdims=True)
    length = jnp.sqrt(jnp.sum(down * down)) * jnp.sqrt(jnp.sum(along * along))
    return jnp.sum(krylov * (down * along)) / length


def signed(n):
    return (n + 1) % 4 - 1


def mod4(at):
    return at[0] % 4, at[1] % 4


PIECES = (("a", 1), ("a", -1), ("b", 1), ("b", -1))
GROUPS = (
    ((1, 0), (0, 1)),
    ((-1, 0), (0, -1)),
    ((1, 1), (-1, -1)),
    ((1, -1), (-1, 1)),
    ((2, 0), (0, 2)),
    ((2, 1), (1, 2)),
    ((2, -1), (-1, 2)),
    ((2, 2),),
)


def onward(piece, source):
    first, sign = piece
    u, v = signed(-source[0]), signed(-source[1])
    if first == "b":
        u, v = v, u
    out = []
    if v == 0:
        if u == 0:
            out += [(1, 0), (-1, 0)]
        elif u == sign:
            out += [(sign, 0)]
        out += [(0, 1), (0, -1)]
    elif v == sign:
        out += [(0, sign)]
    if first == "b":
        out = [(v, u) for u, v in out]
    return out


def slot(at):
    i, j = mod4(at)
    return 4 * i + j


def spans(start, counts):
    out = []
    for count in counts:
        out.append((start, start + count))
        start += count
    return tuple(out)


BANDS = spans(0, (64, 64, 64, 64))


class Flow:
    def __init__(self, wall, rows, recv, send, sib_recv, sib_send, device_at, sibling):
        self.wall, self.rows = wall, rows
        self.recv, self.send, self.sib_recv, self.sib_send = recv, send, sib_recv, sib_send
        self.device_at, self.sibling = device_at, sibling
        self.first, self.last = rows[0][0], rows[-1][1]

    def copies(self, owner, low, high, send, recv, to):
        band = pl.ds(low, high - low)
        pltpu.make_async_remote_copy(
            src_ref=self.wall.at[owner, band],
            dst_ref=self.wall.at[owner, band],
            send_sem=send,
            recv_sem=recv,
            device_id=to,
        ).start()

    def bytes_of(self, count, high_less_low, sem):
        ref = self.wall.at[pl.ds(0, count), pl.ds(0, high_less_low)]
        return pltpu.make_async_remote_copy(
            src_ref=ref, dst_ref=ref, send_sem=sem, recv_sem=sem, device_id=self.sibling
        )

    def pass_on(self, t, owner, source, to):
        low, high = self.rows[t]
        there = self.recv.at[t, slot((source[0] - to[0], source[1] - to[1]))]
        self.copies(owner, low, high, self.send.at[t], there, self.device_at(to))

    def to_sibling(self, owner, source):
        there = self.sib_recv.at[slot((source[1], source[0]))]
        self.copies(owner, self.first, self.last, self.sib_send, there, self.sibling)

    def begin(self, owner):
        for rank in range(4):
            for t, piece in enumerate(PIECES):
                self.pass_on(t, owner, (0, 0), onward(piece, (0, 0))[rank])
        self.to_sibling(owner, (0, 0))

    def events(self, owner, source):
        for t, piece in enumerate(PIECES):
            low, high = self.rows[t]
            self.bytes_of(1, high - low, self.recv.at[t, slot(source)]).wait_recv()
            for to in onward(piece, source):
                self.pass_on(t, owner, source, to)
        self.to_sibling(owner, source)

    def from_sibling(self, owner, source):
        self.bytes_of(1, self.last - self.first, self.sib_recv.at[slot(source)]).wait_recv()

    def sent(self):
        for t, (low, high) in enumerate(self.rows):
            self.bytes_of(15, high - low, self.send.at[t]).wait_send()
        self.bytes_of(16, self.last - self.first, self.sib_send).wait_send()


def step_kernel(
    nf,
    nt,
    tokens_ref,
    weight_hbm,
    probes_ref,
    momentum_hbm,
    gradient_hbm,
    partial_ref,
    last_ref,
    krylov_ref,
    wall,
    acc,
    toks,
    block,
    basis,
    small,
    weight_ref,
    momentum_ref,
    gradient_ref,
    parts,
    gbuf,
    tbuf,
    fsend,
    frecv,
    gathered,
    drecv,
    late_recv,
    late_send,
    late_sib_recv,
    late_sib_send,
    tok_sem,
    out_sem,
    in_sem,
    g_send,
    g_recv,
    t_send,
    t_recv,
    rs_send,
    rs_recv,
    ag_send,
    ag_recv,
    d_send,
    d_recv,
):
    mf = lax.axis_index("fsdp")
    mt = lax.axis_index("tensor")
    rows, cols = momentum_ref.shape
    width = cols // 8
    core = lax.rem(mf, 2)
    chip = lax.div(mf, 2)
    mx, mz = lax.div(chip, 4), lax.rem(chip, 4)

    def chip_at(at):
        i, j = at
        x = lax.rem(mx + 4 + i * (1 - core) + j * core, 4)
        z = lax.rem(mz + 4 + i * core + j * (1 - core), 4)
        return 4 * x + z

    def device_at(at):
        return {"fsdp": 2 * chip_at(at) + core}

    sibling = {"fsdp": 2 * chip + 1 - core}

    def fsdp_at(k):
        return {"fsdp": lax.rem(mf + k, nf)}

    def tensor_at(k):
        return {"tensor": lax.rem(mt + k, nt)}

    loads = [
        pltpu.make_async_copy(source, target, in_sem.at[at])
        for at, (source, target) in enumerate(
            ((momentum_hbm, momentum_ref), (gradient_hbm, gradient_ref), (weight_hbm, weight_ref))
        )
    ]
    for load in loads:
        load.start()
    barrier = pltpu.get_barrier_semaphore()

    @pl.loop(1, nf)
    def _(k):
        pl.semaphore_signal(barrier, inc=1, device_id=fsdp_at(k))

    @pl.loop(1, nt)
    def _(k):
        pl.semaphore_signal(barrier, inc=1, device_id=tensor_at(k))

    lane = lax.broadcasted_iota(jnp.int32, (K, LANES), 1)

    def to_all(src, dst, send, recv):
        for k in range(1, nf):
            pltpu.make_async_remote_copy(
                src_ref=src(lax.rem(mf + k, nf)),
                dst_ref=dst,
                send_sem=send,
                recv_sem=recv,
                device_id=fsdp_at(k),
            ).start()

    def to_tensor(ref, send, recv):
        for k in range(1, nt):
            pltpu.make_async_remote_copy(
                src_ref=ref,
                dst_ref=ref,
                send_sem=send,
                recv_sem=recv,
                device_id=tensor_at(k),
            ).start()

    def all_of(ref, send, recv, count):
        return pltpu.make_async_remote_copy(
            src_ref=ref.at[pl.ds(0, count)],
            dst_ref=ref.at[pl.ds(0, count)],
            send_sem=send,
            recv_sem=recv,
            device_id=fsdp_at(1),
        )

    flow = Flow(wall, BANDS, late_recv, late_send, late_sib_recv, late_sib_send, device_at, sibling)

    def owner_at(source):
        return 2 * chip_at(source) + core

    block[...] = probes_ref[...]
    small[...] = jnp.zeros_like(small)

    def send_gram(step, now):
        small[:, :K] = hdot_t(now, now)
        gbuf[step, mt] = pack(small[...])
        if step == 0:
            pl.semaphore_wait(barrier, nf + nt - 2)
        to_tensor(gbuf.at[step, mt], g_send.at[step], g_recv.at[step])

    send_gram(0, probes_ref[...])
    loads[0].wait()
    loads[1].wait()
    moment = 0.9 * momentum_ref[...] + gradient_ref[...].astype(F32)
    for at, value in enumerate(split(moment)):
        parts[at] = value
    diags, uppers = [], []
    for step in range(STEPS):
        now = block[...]
        if step:
            send_gram(step, now)
        tbuf[step, mt] = split_dot(now, parts, 1)
        to_tensor(tbuf.at[step, mt], t_send.at[step], t_recv.at[step])
        all_of(gbuf.at[step], g_send.at[step], g_recv.at[step], nt - 1).wait_recv()
        gram = gbuf[step, 0]
        for other in range(1, nt):
            gram = gram + gbuf[step, other]
        upper_next, inverse_low = eliminate(unpack(gram))
        if step:
            uppers.append(upper_next)
        all_of(tbuf.at[step], t_send.at[step], t_recv.at[step], nt - 1).wait_recv()
        total = tbuf[step, 0]
        for other in range(1, nt):
            total = total + tbuf[step, other]
        inverse_low = inverse_low[:, :K]
        reduced = hdot(inverse_low, total)
        small[:, :K] = hdot_t(reduced, reduced)
        tile = pack(small[...])
        if step + 1 < STEPS:
            drecv[step, mf] = tile
            images = split_dot(reduced, parts, 0)
            for r in range(4):
                for c in range(8):
                    fsend[step, 8 * r + c] = images[
                        8 * r : 8 * r + 8, width * c : width * (c + 1)
                    ]
            frecv[step, mf] = fsend[step, mf]
            to_all(
                lambda dest: fsend.at[step, dest],
                frecv.at[step, mf],
                rs_send.at[step],
                rs_recv.at[step],
            )
            to_all(
                lambda dest: drecv.at[step, mf], drecv.at[step, mf], d_send.at[step], d_recv.at[step]
            )
            basis[step] = hdot(inverse_low, now)
            all_of(frecv.at[step], rs_send.at[step], rs_recv.at[step], nf - 1).wait_recv()
            summed = jnp.sum(frecv[step], axis=0)
            gathered[step, mf] = summed
            to_all(
                lambda dest: gathered.at[step, mf],
                gathered.at[step, mf],
                ag_send.at[step],
                ag_recv.at[step],
            )
            all_of(drecv.at[step], d_send.at[step], d_recv.at[step], nf - 1).wait_recv()
            diag = unpack(jnp.sum(drecv[step], axis=0))
            rest = hdot(diag[:, :K], basis[step])
            if step:
                rest = rest + hdot(upper_next[:, :K], basis[step - 1])
            block[...] = rest
            all_of(gathered.at[step], ag_send.at[step], ag_recv.at[step], nf - 1).wait_recv()
            for r in range(4):
                for c in range(8):
                    where = (slice(8 * r, 8 * r + 8), slice(width * c, width * (c + 1)))
                    block[where] = gathered[step, 8 * r + c] - block[where]
        else:
            drecv[step, mf] = tile
            to_all(
                lambda dest: drecv.at[step, mf], drecv.at[step, mf], d_send.at[step], d_recv.at[step]
            )
            all_of(drecv.at[step], d_send.at[step], d_recv.at[step], nf - 1).wait_recv()
            diag = unpack(jnp.sum(drecv[step], axis=0))
        diags.append(diag)

    eye = jnp.where(lax.broadcasted_iota(jnp.int32, (K, K), 0) == lax.broadcasted_iota(jnp.int32, (K, K), 1), 1.0, 0.0)
    lows = []
    for at in range(STEPS - 1):
        small[:, :K] = hdot_t(eye, uppers[at][:, :K])
        lows.append(small[...])
    bands = []
    for at in range(STEPS):
        band = pltpu.roll(diags[at], K * at, 1) if at else diags[at]
        if at + 1 < STEPS:
            band = band + pltpu.roll(lows[at], K * (at + 1), 1)
        if at:
            before = uppers[at - 1]
            band = band + (pltpu.roll(before, K * (at - 1), 1) if at > 1 else before)
        bands.append(band)
    bands.append(jnp.zeros((K, LANES), F32))
    krylov = jnp.concatenate(bands, axis=0)
    top = top_value(krylov)
    krylov_ref[...] = krylov / top
    scale = 1.0 / jnp.sqrt(top)
    loads[2].wait()
    fresh = 0.9 * momentum_ref[...] + gradient_ref[...].astype(F32)
    wall[mf] = (weight_ref[...].astype(F32) - fresh * scale).astype(jnp.bfloat16)
    flow.begin(mf)

    order = [(0, 0)] + [source for group in GROUPS for source in group]

    def tokens_of(number):
        columns = pl.ds(pl.multiple_of(chip_at(order[number]) * 2 * rows, 2 * rows), 2 * rows)
        return pltpu.make_async_copy(
            tokens_ref.at[:, columns], toks.at[number % 2], tok_sem.at[number % 2]
        )

    tokens_of(0).start()

    def multiply(source):
        number = order.index(source)
        if number + 2 < len(order):
            tokens_of(number + 1).start()
        left_owner = 2 * chip_at(source)
        flow.from_sibling(left_owner + 1 - core, source)
        tokens_of(number).wait()
        left = toks[number % 2]

        @pl.loop(0, cols // 1024)
        def _(n):
            at = pl.ds(pl.multiple_of(n * 1024, 1024), 1024)
            right = wall[pl.ds(left_owner, 2), :, at].reshape(2 * rows, 1024)
            product = jnp.dot(left, right, preferred_element_type=F32)
            if number:
                acc[:, at] += product
            else:
                acc[:, at] = product

    last = order[-1]
    for number, source in enumerate(order[1:-1]):
        flow.events(owner_at(source), source)
        if number != 1:
            multiply(order[number - (number > 1)])
    multiply(order[-3])
    multiply(order[-2])
    partial = pltpu.make_async_copy(acc, partial_ref, out_sem)
    partial.start()
    flow.events(owner_at(last), last)
    flow.from_sibling(2 * chip_at(last) + 1 - core, last)
    final = pltpu.make_async_copy(wall.at[pl.ds(2 * chip_at(last), 2)], last_ref, tok_sem.at[0])
    final.start()
    flow.sent()
    for step in range(STEPS):
        all_of(gbuf.at[step], g_send.at[step], g_recv.at[step], nt - 1).wait_send()
        all_of(tbuf.at[step], t_send.at[step], t_recv.at[step], nt - 1).wait_send()
        all_of(drecv.at[step], d_send.at[step], d_recv.at[step], nf - 1).wait_send()
        if step + 1 < STEPS:
            all_of(fsend.at[step], rs_send.at[step], rs_recv.at[step], nf - 1).wait_send()
            all_of(gathered.at[step], ag_send.at[step], ag_recv.at[step], nf - 1).wait_send()
    partial.wait()
    final.wait()


def step_call(tokens, weight, momentum, gradient, probes, nf, nt):
    rows, cols = momentum.shape
    width = cols // 8
    count = tokens.shape[0]
    vmem = pl.BlockSpec(memory_space=pltpu.VMEM)
    anywhere = pl.BlockSpec(memory_space=pl.ANY)
    dma = pltpu.SemaphoreType.DMA
    return pl.pallas_call(
        functools.partial(step_kernel, nf, nt),
        out_shape=(
            jax.ShapeDtypeStruct((count, cols), F32),
            jax.ShapeDtypeStruct((2, rows, cols), jnp.bfloat16),
            jax.ShapeDtypeStruct((LANES, LANES), F32),
        ),
        in_specs=[anywhere, anywhere, vmem, anywhere, anywhere],
        out_specs=(anywhere, anywhere, vmem),
        scratch_shapes=[
            pltpu.VMEM((nf, rows, cols), jnp.bfloat16),
            pltpu.VMEM((count, cols), F32),
            pltpu.VMEM((2, count, 2 * rows), jnp.bfloat16),
            pltpu.VMEM((K, cols), F32),
            pltpu.VMEM((STEPS - 1, K, cols), F32),
            pltpu.VMEM((K, LANES), F32),
            pltpu.VMEM((rows, cols), jnp.bfloat16),
            pltpu.VMEM((rows, cols), F32),
            pltpu.VMEM((rows, cols), jnp.bfloat16),
            pltpu.VMEM((3, rows, cols), jnp.bfloat16),
            pltpu.VMEM((STEPS, nt, 8, LANES), F32),
            pltpu.VMEM((STEPS, nt, K, rows), F32),
            pltpu.VMEM((STEPS - 1, nf, 8, width), F32),
            pltpu.VMEM((STEPS - 1, nf, 8, width), F32),
            pltpu.VMEM((STEPS - 1, nf, 8, width), F32),
            pltpu.VMEM((STEPS, nf, 8, LANES), F32),
            dma((4, 16)),
            dma((4,)),
            dma((16,)),
            dma(()),
            dma((2,)),
            dma(()),
            dma((3,)),
            dma((STEPS,)),
            dma((STEPS,)),
            dma((STEPS,)),
            dma((STEPS,)),
            dma((STEPS - 1,)),
            dma((STEPS - 1,)),
            dma((STEPS - 1,)),
            dma((STEPS - 1,)),
            dma((STEPS,)),
            dma((STEPS,)),
        ],
        compiler_params=pltpu.CompilerParams(
            collective_id=0, has_side_effects=True, vmem_limit_bytes=56 * 1024 * 1024
        ),
    )(tokens, weight, probes, momentum, gradient)


def finish_kernel(
    chip_ref,
    partial_ref,
    tokens_ref,
    last_ref,
    momentum_ref,
    gradient_ref,
    krylov_ref,
    out_ref,
    moment_ref,
    scaled_ref,
):
    both, rows, cols = last_ref.shape
    right = last_ref[...].reshape(both * rows, cols)
    out_ref[...] = partial_ref[...] + jnp.dot(tokens_ref[...], right, preferred_element_type=F32)
    moment_ref[...] = 0.9 * momentum_ref[...] + gradient_ref[...].astype(F32)
    size = scaled_ref.shape[0]
    scaled_ref[...] = krylov_ref[:size, :size]


def finish(chip, partial, tokens, last, momentum, gradient, krylov):
    count, cols = partial.shape
    rows = momentum.shape[0]
    turns = 4
    size = STEPS * K
    by_cols = pl.BlockSpec((count, cols // turns), lambda n, chip: (0, n))
    by_rows = pl.BlockSpec((rows // turns, cols), lambda n, chip: (n, 0))
    return pl.pallas_call(
        finish_kernel,
        grid_spec=pltpu.PrefetchScalarGridSpec(
            num_scalar_prefetch=1,
            grid=(turns,),
            in_specs=[
                by_cols,
                pl.BlockSpec((count, 2 * rows), lambda n, chip: (0, chip[0])),
                pl.BlockSpec((2, rows, cols // turns), lambda n, chip: (0, 0, n)),
                by_rows,
                by_rows,
                pl.BlockSpec((LANES, LANES), lambda n, chip: (0, 0)),
            ],
            out_specs=(by_cols, by_rows, pl.BlockSpec((size, size), lambda n, chip: (0, 0))),
        ),
        out_shape=(
            jax.ShapeDtypeStruct((count, cols), F32),
            jax.ShapeDtypeStruct((rows, cols), F32),
            jax.ShapeDtypeStruct((size, size), F32),
        ),
    )(chip, partial, tokens, last, momentum, gradient, krylov)


def local(nf, nt, tokens, weight, momentum, gradient, probes):
    partial, last, krylov = step_call(tokens, weight, momentum, gradient, probes, nf, nt)
    chip = lax.div(lax.axis_index("fsdp"), 2)
    far = 4 * lax.rem(lax.div(chip, 4) + 2, 4) + lax.rem(chip + 2, 4)
    return finish(far.reshape(1), partial, tokens, last, momentum, gradient, krylov)


def solution(mesh):
    return jax.shard_map(
        functools.partial(local, mesh.shape["fsdp"], mesh.shape["tensor"]),
        mesh=mesh,
        in_specs=(
            P("fsdp", None),
            P("fsdp", "tensor"),
            P("fsdp", "tensor"),
            P("fsdp", "tensor"),
            P(None, "tensor"),
        ),
        out_specs=(P("fsdp", "tensor"), P("fsdp", "tensor"), P()),
        check_vma=False,
    )
```

```python
import functools

import jax
import jax.numpy as jnp
from jax import lax
from jax.experimental import pallas as pl
from jax.experimental.pallas import tpu as pltpu
from jax.sharding import PartitionSpec as P

STEPS = 3
K = 32
LANES = 128
HIGHEST = lax.Precision.HIGHEST
F32 = jnp.float32


def hdot(left, right):
    return jnp.dot(left, right, precision=HIGHEST, preferred_element_type=F32)


def hdot_t(left, right):
    return lax.dot_general(
        left, right, (((1,), (1,)), ((), ())), precision=HIGHEST, preferred_element_type=F32
    )


def split(value):
    high = value.astype(jnp.bfloat16)
    rest = value - high.astype(F32)
    middle = rest.astype(jnp.bfloat16)
    return high, middle, (rest - middle.astype(F32)).astype(jnp.bfloat16)


def split_dot(left, right, contract):
    def dot(a, b):
        return lax.dot_general(a, b, (((1,), (contract,)), ((), ())), preferred_element_type=F32)

    high, middle, low = split(left)
    first = dot(jnp.concatenate([high, middle, low], axis=0), right[0])
    second = dot(jnp.concatenate([high, middle], axis=0), right[1])
    third = dot(high, right[2])
    small = first[2 * K :] + second[K:] + third
    return first[:K] + ((first[K : 2 * K] + second[:K]) + small)


def eliminate(gram):
    lane = lax.broadcasted_iota(jnp.int32, (8, LANES), 1)
    sub = lax.broadcasted_iota(jnp.int32, (8, LANES), 0)
    sub_col = lax.broadcasted_iota(jnp.int32, (8, 1), 0)
    count = K // 8
    blocks = []
    for at in range(count):
        eye = jnp.where(lane == sub + (8 * at + K), 1.0, 0.0)
        blocks.append(gram[8 * at : 8 * at + 8, :] + eye)
    for j in range(K):
        at, row = divmod(j, 8)
        pivot_row = blocks[at][row : row + 1, :]
        inverse = 1.0 / blocks[at][row : row + 1, j : j + 1]
        scaled = pivot_row * inverse
        for other in range(at, count):
            column = blocks[other][:, j : j + 1]
            if other == at:
                column = jnp.where(sub_col > row, column, 0.0)
            blocks[other] = blocks[other] - column * scaled
    upper, inverse_low = [], []
    for at in range(count):
        row = sub + 8 * at
        pivots = jnp.sum(jnp.where(lane == row, blocks[at], 0.0), axis=1, keepdims=True)
        scaled = blocks[at] / jnp.sqrt(pivots)
        upper.append(jnp.where((lane >= row) & (lane < K), scaled, 0.0))
        shifted = pltpu.roll(scaled, LANES - K, 1)
        inverse_low.append(jnp.where(lane <= row, shifted, 0.0))
    return jnp.concatenate(upper, axis=0), jnp.concatenate(inverse_low, axis=0)


def pack(square):
    tile = square[0:8, :]
    for at in range(1, K // 8):
        tile = tile + pltpu.roll(square[8 * at : 8 * at + 8, :], K * at, 1)
    return tile


def unpack(tile):
    lane = lax.broadcasted_iota(jnp.int32, (8, LANES), 1)
    parts = []
    for at in range(K // 8):
        part = tile if at == 0 else pltpu.roll(tile, LANES - K * at, 1)
        parts.append(jnp.where(lane < K, part, 0.0))
    return jnp.concatenate(parts, axis=0)


def top_value(krylov):
    def unit(power):
        return power / jnp.max(jnp.abs(power))

    power = unit(krylov)
    for turn in range(5):
        power = hdot(power, power)
        if turn == 2:
            power = unit(power)
    down = jnp.sum(power, axis=1, keepdims=True)
    along = jnp.sum(power, axis=0, keepdims=True)
    length = jnp.sqrt(jnp.sum(down * down)) * jnp.sqrt(jnp.sum(along * along))
    return jnp.sum(krylov * (down * along)) / length


def signed(n):
    return (n + 1) % 4 - 1


def mod4(at):
    return at[0] % 4, at[1] % 4


PIECES = (("a", 1), ("a", -1), ("b", 1), ("b", -1))
GROUPS = (
    ((1, 0), (0, 1)),
    ((-1, 0), (0, -1)),
    ((1, 1), (-1, -1)),
    ((1, -1), (-1, 1)),
    ((2, 0), (0, 2)),
    ((2, 1), (1, 2)),
    ((2, -1), (-1, 2)),
    ((2, 2),),
)


def onward(piece, source):
    first, sign = piece
    u, v = signed(-source[0]), signed(-source[1])
    if first == "b":
        u, v = v, u
    out = []
    if v == 0:
        if u == 0:
            out += [(1, 0), (-1, 0)]
        elif u == sign:
            out += [(sign, 0)]
        out += [(0, 1), (0, -1)]
    elif v == sign:
        out += [(0, sign)]
    if first == "b":
        out = [(v, u) for u, v in out]
    return out


def slot(at):
    i, j = mod4(at)
    return 4 * i + j


def spans(start, counts):
    out = []
    for count in counts:
        out.append((start, start + count))
        start += count
    return tuple(out)


BANDS = spans(0, (64, 64, 64, 64))


PARTNERS = sorted(
    ((i, j, other) for i in (1, 2, -1, 0) for j in (2, 1, -1, 0) for other in (0, 1) if (i, j, other) != (0, 0, 0)),
    key=lambda at: -(abs(at[0]) + abs(at[1])),
)


class Flow:
    def __init__(self, wall, rows, recv, send, sib_recv, sib_send, device_at, sibling):
        self.wall, self.rows = wall, rows
        self.recv, self.send, self.sib_recv, self.sib_send = recv, send, sib_recv, sib_send
        self.device_at, self.sibling = device_at, sibling
        self.first, self.last = rows[0][0], rows[-1][1]

    def copies(self, owner, low, high, send, recv, to):
        band = pl.ds(low, high - low)
        pltpu.make_async_remote_copy(
            src_ref=self.wall.at[owner, band],
            dst_ref=self.wall.at[owner, band],
            send_sem=send,
            recv_sem=recv,
            device_id=to,
        ).start()

    def bytes_of(self, count, high_less_low, sem):
        ref = self.wall.at[pl.ds(0, count), pl.ds(0, high_less_low)]
        return pltpu.make_async_remote_copy(
            src_ref=ref, dst_ref=ref, send_sem=sem, recv_sem=sem, device_id=self.sibling
        )

    def pass_on(self, t, owner, source, to):
        low, high = self.rows[t]
        there = self.recv.at[t, slot((source[0] - to[0], source[1] - to[1]))]
        self.copies(owner, low, high, self.send.at[t], there, self.device_at(to))

    def to_sibling(self, owner, source):
        there = self.sib_recv.at[slot((source[1], source[0]))]
        self.copies(owner, self.first, self.last, self.sib_send, there, self.sibling)

    def begin(self, owner):
        for rank in range(4):
            for t, piece in enumerate(PIECES):
                self.pass_on(t, owner, (0, 0), onward(piece, (0, 0))[rank])
        self.to_sibling(owner, (0, 0))

    def events(self, owner, source):
        for t, piece in enumerate(PIECES):
            low, high = self.rows[t]
            self.bytes_of(1, high - low, self.recv.at[t, slot(source)]).wait_recv()
            for to in onward(piece, source):
                self.pass_on(t, owner, source, to)
        self.to_sibling(owner, source)

    def last_event(self, owner, source):
        for t, (low, high) in enumerate(self.rows):
            self.bytes_of(1, high - low, self.recv.at[t, slot(source)]).wait_recv()
            there = self.sib_recv.at[slot((source[1], source[0]))]
            self.copies(owner, low, high, self.sib_send, there, self.sibling)

    def from_sibling(self, owner, source):
        self.bytes_of(1, self.last - self.first, self.sib_recv.at[slot(source)]).wait_recv()

    def sent(self):
        for t, (low, high) in enumerate(self.rows):
            self.bytes_of(15, high - low, self.send.at[t]).wait_send()
        self.bytes_of(16, self.last - self.first, self.sib_send).wait_send()


def step_kernel(
    nf,
    nt,
    tokens_ref,
    weight_hbm,
    probes_ref,
    momentum_hbm,
    gradient_hbm,
    partial_ref,
    last_ref,
    left_ref,
    krylov_ref,
    wall,
    toks,
    block,
    basis,
    small,
    weight_ref,
    momentum_ref,
    gradient_ref,
    parts,
    gbuf,
    tbuf,
    fsend,
    frecv,
    gathered,
    drecv,
    late_recv,
    late_send,
    late_sib_recv,
    late_sib_send,
    tok_sem,
    in_sem,
    left_sem,
    g_send,
    g_recv,
    t_send,
    t_recv,
    rs_send,
    rs_recv,
    ag_send,
    ag_recv,
    d_send,
    d_recv,
):
    mf = lax.axis_index("fsdp")
    mt = lax.axis_index("tensor")
    rows, cols = momentum_ref.shape
    width = cols // 8
    core = lax.rem(mf, 2)
    chip = lax.div(mf, 2)
    mx, mz = lax.div(chip, 4), lax.rem(chip, 4)

    def chip_at(at):
        i, j = at
        x = lax.rem(mx + 4 + i * (1 - core) + j * core, 4)
        z = lax.rem(mz + 4 + i * core + j * (1 - core), 4)
        return 4 * x + z

    def device_at(at):
        return {"fsdp": 2 * chip_at(at) + core}

    sibling = {"fsdp": 2 * chip + 1 - core}

    def fsdp_at(k):
        return {"fsdp": lax.rem(mf + k, nf)}

    def tensor_at(k):
        return {"tensor": lax.rem(mt + k, nt)}

    loads = [
        pltpu.make_async_copy(source, target, in_sem.at[at])
        for at, (source, target) in enumerate(
            ((momentum_hbm, momentum_ref), (gradient_hbm, gradient_ref), (weight_hbm, weight_ref))
        )
    ]
    for load in loads:
        load.start()
    barrier = pltpu.get_barrier_semaphore()

    @pl.loop(1, nf)
    def _(k):
        pl.semaphore_signal(barrier, inc=1, device_id=fsdp_at(k))

    @pl.loop(1, nt)
    def _(k):
        pl.semaphore_signal(barrier, inc=1, device_id=tensor_at(k))

    lane = lax.broadcasted_iota(jnp.int32, (K, LANES), 1)

    def to_all(src, dst, send, recv):
        for i, j, other in PARTNERS:
            to = 2 * chip_at((i, j)) + (1 - core if other else core)
            pltpu.make_async_remote_copy(
                src_ref=src(to),
                dst_ref=dst,
                send_sem=send,
                recv_sem=recv,
                device_id={"fsdp": to},
            ).start()

    def to_tensor(ref, send, recv):
        for k in (2, 1, 3):
            pltpu.make_async_remote_copy(
                src_ref=ref,
                dst_ref=ref,
                send_sem=send,
                recv_sem=recv,
                device_id=tensor_at(k),
            ).start()

    def all_of(ref, send, recv, count):
        return pltpu.make_async_remote_copy(
            src_ref=ref.at[pl.ds(0, count)],
            dst_ref=ref.at[pl.ds(0, count)],
            send_sem=send,
            recv_sem=recv,
            device_id=fsdp_at(1),
        )

    flow = Flow(wall, BANDS, late_recv, late_send, late_sib_recv, late_sib_send, device_at, sibling)

    def owner_at(source):
        return 2 * chip_at(source) + core

    block[...] = probes_ref[...]
    small[...] = jnp.zeros_like(small)

    def send_gram(step, now):
        small[:, :K] = hdot_t(now, now)
        gbuf[step, mt] = pack(small[...])
        if step == 0:
            pl.semaphore_wait(barrier, nf + nt - 2)
        to_tensor(gbuf.at[step, mt], g_send.at[step], g_recv.at[step])

    send_gram(0, probes_ref[...])
    loads[0].wait()
    loads[1].wait()
    moment = 0.9 * momentum_ref[...] + gradient_ref[...].astype(F32)
    for at, value in enumerate(split(moment)):
        parts[at] = value
    diags, uppers = [], []
    for step in range(STEPS):
        now = block[...]
        if step:
            send_gram(step, now)
        tbuf[step, mt] = split_dot(now, parts, 1)
        to_tensor(tbuf.at[step, mt], t_send.at[step], t_recv.at[step])
        all_of(gbuf.at[step], g_send.at[step], g_recv.at[step], nt - 1).wait_recv()
        gram = gbuf[step, 0]
        for other in range(1, nt):
            gram = gram + gbuf[step, other]
        upper_next, inverse_low = eliminate(unpack(gram))
        if step:
            uppers.append(upper_next)
        all_of(tbuf.at[step], t_send.at[step], t_recv.at[step], nt - 1).wait_recv()
        total = tbuf[step, 0]
        for other in range(1, nt):
            total = total + tbuf[step, other]
        inverse_low = inverse_low[:, :K]
        reduced = hdot(inverse_low, total)
        small[:, :K] = hdot_t(reduced, reduced)
        tile = pack(small[...])
        if step + 1 < STEPS:
            drecv[step, mf] = tile
            images = split_dot(reduced, parts, 0)
            for r in range(4):
                for c in range(8):
                    fsend[step, 8 * r + c] = images[
                        8 * r : 8 * r + 8, width * c : width * (c + 1)
                    ]
            frecv[step, mf] = fsend[step, mf]
            to_all(
                lambda dest: fsend.at[step, dest],
                frecv.at[step, mf],
                rs_send.at[step],
                rs_recv.at[step],
            )
            to_all(
                lambda dest: drecv.at[step, mf], drecv.at[step, mf], d_send.at[step], d_recv.at[step]
            )
            basis[step] = hdot(inverse_low, now)
            all_of(frecv.at[step], rs_send.at[step], rs_recv.at[step], nf - 1).wait_recv()
            summed = jnp.sum(frecv[step], axis=0)
            gathered[step, mf] = summed
            to_all(
                lambda dest: gathered.at[step, mf],
                gathered.at[step, mf],
                ag_send.at[step],
                ag_recv.at[step],
            )
            all_of(drecv.at[step], d_send.at[step], d_recv.at[step], nf - 1).wait_recv()
            diag = unpack(jnp.sum(drecv[step], axis=0))
            rest = hdot(diag[:, :K], basis[step])
            if step:
                rest = rest + hdot(upper_next[:, :K], basis[step - 1])
            block[...] = rest
            all_of(gathered.at[step], ag_send.at[step], ag_recv.at[step], nf - 1).wait_recv()
            for r in range(4):
                for c in range(8):
                    where = (slice(8 * r, 8 * r + 8), slice(width * c, width * (c + 1)))
                    block[where] = gathered[step, 8 * r + c] - block[where]
        else:
            drecv[step, mf] = tile
            to_all(
                lambda dest: drecv.at[step, mf], drecv.at[step, mf], d_send.at[step], d_recv.at[step]
            )
            all_of(drecv.at[step], d_send.at[step], d_recv.at[step], nf - 1).wait_recv()
            diag = unpack(jnp.sum(drecv[step], axis=0))
        diags.append(diag)

    eye = jnp.where(lax.broadcasted_iota(jnp.int32, (K, K), 0) == lax.broadcasted_iota(jnp.int32, (K, K), 1), 1.0, 0.0)
    lows = []
    for at in range(STEPS - 1):
        small[:, :K] = hdot_t(eye, uppers[at][:, :K])
        lows.append(small[...])
    bands = []
    for at in range(STEPS):
        band = pltpu.roll(diags[at], K * at, 1) if at else diags[at]
        if at + 1 < STEPS:
            band = band + pltpu.roll(lows[at], K * (at + 1), 1)
        if at:
            before = uppers[at - 1]
            band = band + (pltpu.roll(before, K * (at - 1), 1) if at > 1 else before)
        bands.append(band)
    bands.append(jnp.zeros((K, LANES), F32))
    krylov = jnp.concatenate(bands, axis=0)
    top = top_value(krylov)
    krylov_ref[...] = krylov / top
    scale = 1.0 / jnp.sqrt(top)
    loads[2].wait()
    fresh = 0.9 * momentum_ref[...] + gradient_ref[...].astype(F32)
    wall[mf] = (weight_ref[...].astype(F32) - fresh * scale).astype(jnp.bfloat16)
    flow.begin(mf)

    order = [(0, 0)] + [source for group in GROUPS for source in group]

    def tokens_of(number):
        columns = pl.ds(pl.multiple_of(chip_at(order[number]) * 2 * rows, 2 * rows), 2 * rows)
        return pltpu.make_async_copy(
            tokens_ref.at[:, columns], toks.at[number % 2], tok_sem.at[number % 2]
        )

    tokens_of(0).start()
    columns = pl.ds(pl.multiple_of(chip_at(order[-1]) * 2 * rows, 2 * rows), 2 * rows)
    final = pltpu.make_async_copy(tokens_ref.at[:, columns], left_ref, left_sem)
    final.start()

    def multiply(source):
        number = order.index(source)
        if number + 2 < len(order):
            tokens_of(number + 1).start()
        left_owner = 2 * chip_at(source)
        flow.from_sibling(left_owner + 1 - core, source)
        tokens_of(number).wait()
        left = toks[number % 2]

        @pl.loop(0, cols // 1024)
        def _(n):
            at = pl.ds(pl.multiple_of(n * 1024, 1024), 1024)
            right = wall[pl.ds(left_owner, 2), :, at].reshape(2 * rows, 1024)
            product = jnp.dot(left, right, preferred_element_type=F32)
            if number:
                partial_ref[:, at] += product
            else:
                partial_ref[:, at] = product

    last = order[-1]
    for number, source in enumerate(order[1:-1]):
        flow.events(owner_at(source), source)
        if number != 1:
            multiply(order[number - (number > 1)])
    multiply(order[-3])
    multiply(order[-2])
    flow.last_event(owner_at(last), last)
    flow.from_sibling(2 * chip_at(last) + 1 - core, last)
    last_ref[...] = wall[pl.ds(2 * chip_at(last), 2)]
    final.wait()
    flow.sent()
    for step in range(STEPS):
        all_of(gbuf.at[step], g_send.at[step], g_recv.at[step], nt - 1).wait_send()
        all_of(tbuf.at[step], t_send.at[step], t_recv.at[step], nt - 1).wait_send()
        all_of(drecv.at[step], d_send.at[step], d_recv.at[step], nf - 1).wait_send()
        if step + 1 < STEPS:
            all_of(fsend.at[step], rs_send.at[step], rs_recv.at[step], nf - 1).wait_send()
            all_of(gathered.at[step], ag_send.at[step], ag_recv.at[step], nf - 1).wait_send()


def step_call(tokens, weight, momentum, gradient, probes, nf, nt):
    rows, cols = momentum.shape
    width = cols // 8
    count = tokens.shape[0]
    vmem = pl.BlockSpec(memory_space=pltpu.VMEM)
    anywhere = pl.BlockSpec(memory_space=pl.ANY)
    dma = pltpu.SemaphoreType.DMA
    return pl.pallas_call(
        functools.partial(step_kernel, nf, nt),
        out_shape=(
            pltpu.VMEM((count, cols), F32),
            pltpu.VMEM((2, rows, cols), jnp.bfloat16),
            pltpu.VMEM((count, 2 * rows), jnp.bfloat16),
            pltpu.VMEM((LANES, LANES), F32),
        ),
        in_specs=[anywhere, anywhere, vmem, anywhere, anywhere],
        out_specs=(vmem, vmem, vmem, vmem),
        scratch_shapes=[
            pltpu.VMEM((nf, rows, cols), jnp.bfloat16),
            pltpu.VMEM((2, count, 2 * rows), jnp.bfloat16),
            pltpu.VMEM((K, cols), F32),
            pltpu.VMEM((STEPS - 1, K, cols), F32),
            pltpu.VMEM((K, LANES), F32),
            pltpu.VMEM((rows, cols), jnp.bfloat16),
            pltpu.VMEM((rows, cols), F32),
            pltpu.VMEM((rows, cols), jnp.bfloat16),
            pltpu.VMEM((3, rows, cols), jnp.bfloat16),
            pltpu.VMEM((STEPS, nt, 8, LANES), F32),
            pltpu.VMEM((STEPS, nt, K, rows), F32),
            pltpu.VMEM((STEPS - 1, nf, 8, width), F32),
            pltpu.VMEM((STEPS - 1, nf, 8, width), F32),
            pltpu.VMEM((STEPS - 1, nf, 8, width), F32),
            pltpu.VMEM((STEPS, nf, 8, LANES), F32),
            dma((4, 16)),
            dma((4,)),
            dma((16,)),
            dma(()),
            dma((2,)),
            dma((3,)),
            dma(()),
            dma((STEPS,)),
            dma((STEPS,)),
            dma((STEPS,)),
            dma((STEPS,)),
            dma((STEPS - 1,)),
            dma((STEPS - 1,)),
            dma((STEPS - 1,)),
            dma((STEPS - 1,)),
            dma((STEPS,)),
            dma((STEPS,)),
        ],
        compiler_params=pltpu.CompilerParams(
            collective_id=0, has_side_effects=True, vmem_limit_bytes=48 * 1024 * 1024
        ),
    )(tokens, weight, probes, momentum, gradient)


def finish_kernel(
    partial_ref,
    left_ref,
    last_ref,
    momentum_ref,
    gradient_ref,
    krylov_ref,
    out_ref,
    moment_ref,
    scaled_ref,
):
    both, rows, cols = last_ref.shape
    width = out_ref.shape[1]
    at = pl.ds(pl.multiple_of(pl.program_id(0) * width, width), width)
    right = last_ref[:, :, at].reshape(both * rows, width)
    out_ref[...] = partial_ref[:, at] + jnp.dot(left_ref[...], right, preferred_element_type=F32)
    moment_ref[...] = 0.9 * momentum_ref[...] + gradient_ref[...].astype(F32)
    size = scaled_ref.shape[0]
    scaled_ref[...] = krylov_ref[:size, :size]


def finish(partial, left, last, momentum, gradient, krylov):
    count, cols = partial.shape
    rows = momentum.shape[0]
    turns = 4
    size = STEPS * K
    vmem = pl.BlockSpec(memory_space=pltpu.VMEM)
    by_cols = pl.BlockSpec((count, cols // turns), lambda n: (0, n))
    by_rows = pl.BlockSpec((rows // turns, cols), lambda n: (n, 0))
    return pl.pallas_call(
        finish_kernel,
        grid=(turns,),
        in_specs=[vmem, vmem, vmem, by_rows, by_rows, vmem],
        out_specs=(by_cols, by_rows, pl.BlockSpec((size, size), lambda n: (0, 0))),
        out_shape=(
            jax.ShapeDtypeStruct((count, cols), F32),
            jax.ShapeDtypeStruct((rows, cols), F32),
            jax.ShapeDtypeStruct((size, size), F32),
        ),
        compiler_params=pltpu.CompilerParams(vmem_limit_bytes=24 * 1024 * 1024),
    )(partial, left, last, momentum, gradient, krylov)


def local(nf, nt, tokens, weight, momentum, gradient, probes):
    held = step_call(tokens, weight, momentum, gradient, probes, nf, nt)
    partial, last, left, krylov = (
        pltpu.with_memory_space_constraint(value, pltpu.VMEM) for value in held
    )
    return finish(partial, left, last, momentum, gradient, krylov)


def solution(mesh):
    return jax.shard_map(
        functools.partial(local, mesh.shape["fsdp"], mesh.shape["tensor"]),
        mesh=mesh,
        in_specs=(
            P("fsdp", None),
            P("fsdp", "tensor"),
            P("fsdp", "tensor"),
            P("fsdp", "tensor"),
            P(None, "tensor"),
        ),
        out_specs=(P("fsdp", "tensor"), P("fsdp", "tensor"), P()),
        check_vma=False,
    )
```

```python
import functools

import jax
import jax.numpy as jnp
from jax import lax
from jax.experimental import pallas as pl
from jax.experimental.pallas import tpu as pltpu
from jax.sharding import PartitionSpec as P

STEPS = 3
K = 32
LANES = 128
HIGHEST = lax.Precision.HIGHEST
F32 = jnp.float32


def hdot(left, right):
    return jnp.dot(left, right, precision=HIGHEST, preferred_element_type=F32)


def hdot_t(left, right):
    return lax.dot_general(
        left, right, (((1,), (1,)), ((), ())), precision=HIGHEST, preferred_element_type=F32
    )


def split(value):
    high = value.astype(jnp.bfloat16)
    rest = value - high.astype(F32)
    middle = rest.astype(jnp.bfloat16)
    return high, middle, (rest - middle.astype(F32)).astype(jnp.bfloat16)


def split_dot(left, right, contract):
    def dot(a, b):
        return lax.dot_general(a, b, (((1,), (contract,)), ((), ())), preferred_element_type=F32)

    high, middle, low = split(left)
    first = dot(jnp.concatenate([high, middle, low], axis=0), right[0])
    second = dot(jnp.concatenate([high, middle], axis=0), right[1])
    third = dot(high, right[2])
    small = first[2 * K :] + second[K:] + third
    return first[:K] + ((first[K : 2 * K] + second[:K]) + small)


def eliminate(gram):
    lane = lax.broadcasted_iota(jnp.int32, (8, LANES), 1)
    sub = lax.broadcasted_iota(jnp.int32, (8, LANES), 0)
    sub_col = lax.broadcasted_iota(jnp.int32, (8, 1), 0)
    count = K // 8
    blocks = []
    for at in range(count):
        eye = jnp.where(lane == sub + (8 * at + K), 1.0, 0.0)
        blocks.append(gram[8 * at : 8 * at + 8, :] + eye)
    for j in range(K):
        at, row = divmod(j, 8)
        pivot_row = blocks[at][row : row + 1, :]
        inverse = 1.0 / blocks[at][row : row + 1, j : j + 1]
        scaled = pivot_row * inverse
        for other in range(at, count):
            column = blocks[other][:, j : j + 1]
            if other == at:
                column = jnp.where(sub_col > row, column, 0.0)
            blocks[other] = blocks[other] - column * scaled
    upper, inverse_low = [], []
    for at in range(count):
        row = sub + 8 * at
        pivots = jnp.sum(jnp.where(lane == row, blocks[at], 0.0), axis=1, keepdims=True)
        scaled = blocks[at] / jnp.sqrt(pivots)
        upper.append(jnp.where((lane >= row) & (lane < K), scaled, 0.0))
        shifted = pltpu.roll(scaled, LANES - K, 1)
        inverse_low.append(jnp.where(lane <= row, shifted, 0.0))
    return jnp.concatenate(upper, axis=0), jnp.concatenate(inverse_low, axis=0)


def pack(square):
    tile = square[0:8, :]
    for at in range(1, K // 8):
        tile = tile + pltpu.roll(square[8 * at : 8 * at + 8, :], K * at, 1)
    return tile


def unpack(tile):
    lane = lax.broadcasted_iota(jnp.int32, (8, LANES), 1)
    parts = []
    for at in range(K // 8):
        part = tile if at == 0 else pltpu.roll(tile, LANES - K * at, 1)
        parts.append(jnp.where(lane < K, part, 0.0))
    return jnp.concatenate(parts, axis=0)


def top_value(krylov):
    def unit(power):
        return power / jnp.max(jnp.abs(power))

    power = unit(krylov)
    for turn in range(5):
        power = hdot(power, power)
        if turn == 2:
            power = unit(power)
    down = jnp.sum(power, axis=1, keepdims=True)
    along = jnp.sum(power, axis=0, keepdims=True)
    length = jnp.sqrt(jnp.sum(down * down)) * jnp.sqrt(jnp.sum(along * along))
    return jnp.sum(krylov * (down * along)) / length


def signed(n):
    return (n + 1) % 4 - 1


def mod4(at):
    return at[0] % 4, at[1] % 4


PIECES = (("a", 1), ("a", -1), ("b", 1), ("b", -1))
LAST = (2, 2)
ORDER = (
    (0, 0), (1, 0), (0, 1), (-1, 0), (0, -1), (1, 1), (-1, -1), (1, -1), (-1, 1),
    (2, 0), (0, 2), (2, 1), (1, 2), (2, -1), (-1, 2), LAST,
)


def onward(piece, source):
    first, sign = piece
    u, v = signed(-source[0]), signed(-source[1])
    if first == "b":
        u, v = v, u
    out = []
    if v == 0:
        if u == 0:
            out += [(1, 0), (-1, 0)]
        elif u == sign:
            out += [(sign, 0)]
        out += [(0, 1), (0, -1)]
    elif v == sign:
        out += [(0, sign)]
    if first == "b":
        out = [(v, u) for u, v in out]
    return out


def level(*places):
    out = []
    for u, v in places:
        for t, (first, sign) in enumerate(PIECES):
            at = (-u * sign, -v * sign)
            at = at if first == "a" else at[::-1]
            out.append((t, (signed(at[0]), signed(at[1]))))
    return out


PLAN = (
    (level((1, 0), (-1, 0)), ((0, 0),)),
    (level((0, 1), (0, -1)), ()),
    (level((2, 0)), ((1, 0),)),
    (level((1, 1), (-1, 1)), ((0, 1),)),
    (level((1, -1), (-1, -1)), ((-1, 0),)),
    (level((2, 1)), ((0, -1),)),
    (level((0, 2)), ((1, 1),)),
    (level((1, 2)), ((-1, -1), (1, -1))),
    (level((-1, 2)), ((-1, 1), (2, 0))),
    (level((2, -1)), ((0, 2), (2, 1), (1, 2), (2, -1), (-1, 2))),
)


def slot(at):
    i, j = mod4(at)
    return 4 * i + j


def spans(start, counts):
    out = []
    for count in counts:
        out.append((start, start + count))
        start += count
    return tuple(out)


BANDS = spans(0, (64, 64, 64, 64))


PARTNERS = sorted(
    ((i, j, other) for i in (1, 2, -1, 0) for j in (2, 1, -1, 0) for other in (0, 1) if (i, j, other) != (0, 0, 0)),
    key=lambda at: -(abs(at[0]) + abs(at[1])),
)


class Flow:
    def __init__(self, wall, rows, recv, send, sib_recv, sib_send, device_at, sibling):
        self.wall, self.rows = wall, rows
        self.recv, self.send, self.sib_recv, self.sib_send = recv, send, sib_recv, sib_send
        self.device_at, self.sibling = device_at, sibling
        self.first, self.last = rows[0][0], rows[-1][1]

    def copies(self, owner, low, high, send, recv, to):
        band = pl.ds(low, high - low)
        pltpu.make_async_remote_copy(
            src_ref=self.wall.at[owner, band],
            dst_ref=self.wall.at[owner, band],
            send_sem=send,
            recv_sem=recv,
            device_id=to,
        ).start()

    def bytes_of(self, count, high_less_low, sem):
        ref = self.wall.at[pl.ds(0, count), pl.ds(0, high_less_low)]
        return pltpu.make_async_remote_copy(
            src_ref=ref, dst_ref=ref, send_sem=sem, recv_sem=sem, device_id=self.sibling
        )

    def pass_on(self, t, owner, source, to):
        low, high = self.rows[t]
        there = self.recv.at[t, slot((source[0] - to[0], source[1] - to[1]))]
        self.copies(owner, low, high, self.send.at[t], there, self.device_at(to))

    def to_sibling(self, owner, source):
        there = self.sib_recv.at[slot((source[1], source[0]))]
        self.copies(owner, self.first, self.last, self.sib_send, there, self.sibling)

    def begin(self, t, owner):
        for to in onward(PIECES[t], (0, 0)):
            self.pass_on(t, owner, (0, 0), to)

    def event(self, t, owner, source):
        low, high = self.rows[t]
        self.bytes_of(1, high - low, self.recv.at[t, slot(source)]).wait_recv()
        for to in onward(PIECES[t], source):
            self.pass_on(t, owner, source, to)

    def last_event(self, owner, source):
        for t, (low, high) in enumerate(self.rows):
            self.bytes_of(1, high - low, self.recv.at[t, slot(source)]).wait_recv()
            there = self.sib_recv.at[slot((source[1], source[0]))]
            self.copies(owner, low, high, self.sib_send, there, self.sibling)

    def from_sibling(self, owner, source):
        self.bytes_of(1, self.last - self.first, self.sib_recv.at[slot(source)]).wait_recv()

    def sent(self):
        for t, (low, high) in enumerate(self.rows):
            self.bytes_of(15, high - low, self.send.at[t]).wait_send()
        self.bytes_of(16, self.last - self.first, self.sib_send).wait_send()


def step_kernel(
    nf,
    nt,
    tokens_ref,
    weight_hbm,
    probes_ref,
    momentum_hbm,
    gradient_hbm,
    partial_ref,
    last_ref,
    left_ref,
    krylov_ref,
    wall,
    toks,
    block,
    basis,
    small,
    weight_ref,
    momentum_ref,
    gradient_ref,
    parts,
    gbuf,
    tbuf,
    fsend,
    frecv,
    gathered,
    drecv,
    late_recv,
    late_send,
    late_sib_recv,
    late_sib_send,
    tok_sem,
    in_sem,
    left_sem,
    g_send,
    g_recv,
    t_send,
    t_recv,
    rs_send,
    rs_recv,
    ag_send,
    ag_recv,
    d_send,
    d_recv,
):
    mf = lax.axis_index("fsdp")
    mt = lax.axis_index("tensor")
    rows, cols = momentum_ref.shape
    width = cols // 8
    core = lax.rem(mf, 2)
    chip = lax.div(mf, 2)
    mx, mz = lax.div(chip, 4), lax.rem(chip, 4)

    def chip_at(at):
        i, j = at
        x = lax.rem(mx + 4 + i * (1 - core) + j * core, 4)
        z = lax.rem(mz + 4 + i * core + j * (1 - core), 4)
        return 4 * x + z

    def device_at(at):
        return {"fsdp": 2 * chip_at(at) + core}

    sibling = {"fsdp": 2 * chip + 1 - core}

    def fsdp_at(k):
        return {"fsdp": lax.rem(mf + k, nf)}

    def tensor_at(k):
        return {"tensor": lax.rem(mt + k, nt)}

    loads = [
        pltpu.make_async_copy(source, target, in_sem.at[at])
        for at, (source, target) in enumerate(
            ((momentum_hbm, momentum_ref), (gradient_hbm, gradient_ref), (weight_hbm, weight_ref))
        )
    ]
    for load in loads:
        load.start()
    barrier = pltpu.get_barrier_semaphore()

    @pl.loop(1, nf)
    def _(k):
        pl.semaphore_signal(barrier, inc=1, device_id=fsdp_at(k))

    @pl.loop(1, nt)
    def _(k):
        pl.semaphore_signal(barrier, inc=1, device_id=tensor_at(k))

    lane = lax.broadcasted_iota(jnp.int32, (K, LANES), 1)

    def to_all(src, dst, send, recv):
        for i, j, other in PARTNERS:
            to = 2 * chip_at((i, j)) + (1 - core if other else core)
            pltpu.make_async_remote_copy(
                src_ref=src(to),
                dst_ref=dst,
                send_sem=send,
                recv_sem=recv,
                device_id={"fsdp": to},
            ).start()

    def to_tensor(ref, send, recv):
        for k in (2, 1, 3):
            pltpu.make_async_remote_copy(
                src_ref=ref,
                dst_ref=ref,
                send_sem=send,
                recv_sem=recv,
                device_id=tensor_at(k),
            ).start()

    def all_of(ref, send, recv, count):
        return pltpu.make_async_remote_copy(
            src_ref=ref.at[pl.ds(0, count)],
            dst_ref=ref.at[pl.ds(0, count)],
            send_sem=send,
            recv_sem=recv,
            device_id=fsdp_at(1),
        )

    flow = Flow(wall, BANDS, late_recv, late_send, late_sib_recv, late_sib_send, device_at, sibling)

    def owner_at(source):
        return 2 * chip_at(source) + core

    block[...] = probes_ref[...]
    small[...] = jnp.zeros_like(small)

    def send_gram(step, now):
        small[:, :K] = hdot_t(now, now)
        gbuf[step, mt] = pack(small[...])
        if step == 0:
            pl.semaphore_wait(barrier, nf + nt - 2)
        to_tensor(gbuf.at[step, mt], g_send.at[step], g_recv.at[step])

    loads[0].wait()
    loads[1].wait()
    moment = 0.9 * momentum_ref[...] + gradient_ref[...].astype(F32)
    for at, value in enumerate(split(moment)):
        parts[at] = value
    send_gram(0, probes_ref[...])
    diags, uppers = [], []
    for step in range(STEPS):
        now = block[...]
        if step:
            send_gram(step, now)
        tbuf[step, mt] = split_dot(now, parts, 1)
        to_tensor(tbuf.at[step, mt], t_send.at[step], t_recv.at[step])
        all_of(gbuf.at[step], g_send.at[step], g_recv.at[step], nt - 1).wait_recv()
        gram = gbuf[step, 0]
        for other in range(1, nt):
            gram = gram + gbuf[step, other]
        upper_next, inverse_low = eliminate(unpack(gram))
        if step:
            uppers.append(upper_next)
        all_of(tbuf.at[step], t_send.at[step], t_recv.at[step], nt - 1).wait_recv()
        total = tbuf[step, 0]
        for other in range(1, nt):
            total = total + tbuf[step, other]
        inverse_low = inverse_low[:, :K]
        reduced = hdot(inverse_low, total)
        small[:, :K] = hdot_t(reduced, reduced)
        tile = pack(small[...])
        if step + 1 < STEPS:
            drecv[step, mf] = tile
            images = split_dot(reduced, parts, 0)
            for r in range(4):
                for c in range(8):
                    fsend[step, 8 * r + c] = images[
                        8 * r : 8 * r + 8, width * c : width * (c + 1)
                    ]
            frecv[step, mf] = fsend[step, mf]
            to_all(
                lambda dest: fsend.at[step, dest],
                frecv.at[step, mf],
                rs_send.at[step],
                rs_recv.at[step],
            )
            to_all(
                lambda dest: drecv.at[step, mf], drecv.at[step, mf], d_send.at[step], d_recv.at[step]
            )
            basis[step] = hdot(inverse_low, now)
            all_of(frecv.at[step], rs_send.at[step], rs_recv.at[step], nf - 1).wait_recv()
            summed = jnp.sum(frecv[step], axis=0)
            gathered[step, mf] = summed
            to_all(
                lambda dest: gathered.at[step, mf],
                gathered.at[step, mf],
                ag_send.at[step],
                ag_recv.at[step],
            )
            all_of(drecv.at[step], d_send.at[step], d_recv.at[step], nf - 1).wait_recv()
            diag = unpack(jnp.sum(drecv[step], axis=0))
            rest = hdot(diag[:, :K], basis[step])
            if step:
                rest = rest + hdot(upper_next[:, :K], basis[step - 1])
            block[...] = rest
            all_of(gathered.at[step], ag_send.at[step], ag_recv.at[step], nf - 1).wait_recv()
            for r in range(4):
                for c in range(8):
                    where = (slice(8 * r, 8 * r + 8), slice(width * c, width * (c + 1)))
                    block[where] = gathered[step, 8 * r + c] - block[where]
        else:
            drecv[step, mf] = tile
            to_all(
                lambda dest: drecv.at[step, mf], drecv.at[step, mf], d_send.at[step], d_recv.at[step]
            )
            row = lax.broadcasted_iota(jnp.int32, (K, K), 0)
            eye = jnp.where(row == lax.broadcasted_iota(jnp.int32, (K, K), 1), 1.0, 0.0)
            lows = []
            for at in range(STEPS - 1):
                small[:, :K] = hdot_t(eye, uppers[at][:, :K])
                lows.append(small[...])
            bands = [
                diags[0] + pltpu.roll(lows[0], K, 1),
                uppers[0] + pltpu.roll(diags[1], K, 1) + pltpu.roll(lows[1], 2 * K, 1),
                pltpu.roll(uppers[1], K, 1),
                jnp.zeros((K, LANES), F32),
            ]
            all_of(drecv.at[step], d_send.at[step], d_recv.at[step], nf - 1).wait_recv()
            diag = unpack(jnp.sum(drecv[step], axis=0))
            bands[2] = bands[2] + pltpu.roll(diag, 2 * K, 1)
        diags.append(diag)

    krylov = jnp.concatenate(bands, axis=0)
    top = top_value(krylov)
    krylov_ref[...] = krylov / top
    scale = 1.0 / jnp.sqrt(top)
    loads[2].wait()
    for t, (low, high) in enumerate(BANDS):
        fresh = 0.9 * momentum_ref[low:high] + gradient_ref[low:high].astype(F32)
        fresh = weight_ref[low:high].astype(F32) - fresh * scale
        wall[mf, low:high] = fresh.astype(jnp.bfloat16)
        flow.begin(t, mf)
    flow.to_sibling(mf, (0, 0))

    order = list(ORDER)

    def tokens_of(number):
        columns = pl.ds(pl.multiple_of(chip_at(order[number]) * 2 * rows, 2 * rows), 2 * rows)
        return pltpu.make_async_copy(
            tokens_ref.at[:, columns], toks.at[number % 2], tok_sem.at[number % 2]
        )

    tokens_of(0).start()
    columns = pl.ds(pl.multiple_of(chip_at(order[-1]) * 2 * rows, 2 * rows), 2 * rows)
    final = pltpu.make_async_copy(tokens_ref.at[:, columns], left_ref, left_sem)
    final.start()

    def multiply(source):
        number = order.index(source)
        if number + 2 < len(order):
            tokens_of(number + 1).start()
        left_owner = 2 * chip_at(source)
        flow.from_sibling(left_owner + 1 - core, source)
        tokens_of(number).wait()
        left = toks[number % 2]

        @pl.loop(0, cols // 1024)
        def _(n):
            at = pl.ds(pl.multiple_of(n * 1024, 1024), 1024)
            right = wall[pl.ds(left_owner, 2), :, at].reshape(2 * rows, 1024)
            product = jnp.dot(left, right, preferred_element_type=F32)
            if number:
                partial_ref[:, at] += product
            else:
                partial_ref[:, at] = product

    seen = {}
    for events, ready in PLAN:
        for t, source in events:
            flow.event(t, owner_at(source), source)
            seen[source] = seen.get(source, 0) + 1
            if seen[source] == len(PIECES):
                flow.to_sibling(owner_at(source), source)
        for source in ready:
            multiply(source)
    last = LAST
    flow.last_event(owner_at(last), last)
    flow.from_sibling(2 * chip_at(last) + 1 - core, last)
    last_ref[...] = wall[pl.ds(2 * chip_at(last), 2)]
    final.wait()
    flow.sent()
    for step in range(STEPS):
        all_of(gbuf.at[step], g_send.at[step], g_recv.at[step], nt - 1).wait_send()
        all_of(tbuf.at[step], t_send.at[step], t_recv.at[step], nt - 1).wait_send()
        all_of(drecv.at[step], d_send.at[step], d_recv.at[step], nf - 1).wait_send()
        if step + 1 < STEPS:
            all_of(fsend.at[step], rs_send.at[step], rs_recv.at[step], nf - 1).wait_send()
            all_of(gathered.at[step], ag_send.at[step], ag_recv.at[step], nf - 1).wait_send()


def step_call(tokens, weight, momentum, gradient, probes, nf, nt):
    rows, cols = momentum.shape
    width = cols // 8
    count = tokens.shape[0]
    vmem = pl.BlockSpec(memory_space=pltpu.VMEM)
    anywhere = pl.BlockSpec(memory_space=pl.ANY)
    dma = pltpu.SemaphoreType.DMA
    return pl.pallas_call(
        functools.partial(step_kernel, nf, nt),
        out_shape=(
            pltpu.VMEM((count, cols), F32),
            pltpu.VMEM((2, rows, cols), jnp.bfloat16),
            pltpu.VMEM((count, 2 * rows), jnp.bfloat16),
            pltpu.VMEM((LANES, LANES), F32),
        ),
        in_specs=[anywhere, anywhere, vmem, anywhere, anywhere],
        out_specs=(vmem, vmem, vmem, vmem),
        scratch_shapes=[
            pltpu.VMEM((nf, rows, cols), jnp.bfloat16),
            pltpu.VMEM((2, count, 2 * rows), jnp.bfloat16),
            pltpu.VMEM((K, cols), F32),
            pltpu.VMEM((STEPS - 1, K, cols), F32),
            pltpu.VMEM((K, LANES), F32),
            pltpu.VMEM((rows, cols), jnp.bfloat16),
            pltpu.VMEM((rows, cols), F32),
            pltpu.VMEM((rows, cols), jnp.bfloat16),
            pltpu.VMEM((3, rows, cols), jnp.bfloat16),
            pltpu.VMEM((STEPS, nt, 8, LANES), F32),
            pltpu.VMEM((STEPS, nt, K, rows), F32),
            pltpu.VMEM((STEPS - 1, nf, 8, width), F32),
            pltpu.VMEM((STEPS - 1, nf, 8, width), F32),
            pltpu.VMEM((STEPS - 1, nf, 8, width), F32),
            pltpu.VMEM((STEPS, nf, 8, LANES), F32),
            dma((4, 16)),
            dma((4,)),
            dma((16,)),
            dma(()),
            dma((2,)),
            dma((3,)),
            dma(()),
            dma((STEPS,)),
            dma((STEPS,)),
            dma((STEPS,)),
            dma((STEPS,)),
            dma((STEPS - 1,)),
            dma((STEPS - 1,)),
            dma((STEPS - 1,)),
            dma((STEPS - 1,)),
            dma((STEPS,)),
            dma((STEPS,)),
        ],
        compiler_params=pltpu.CompilerParams(
            collective_id=0, has_side_effects=True, vmem_limit_bytes=48 * 1024 * 1024
        ),
    )(tokens, weight, probes, momentum, gradient)


def finish_kernel(
    partial_ref,
    left_ref,
    last_ref,
    momentum_ref,
    gradient_ref,
    krylov_ref,
    out_ref,
    moment_ref,
    scaled_ref,
):
    both, rows, cols = last_ref.shape
    width = out_ref.shape[1]
    at = pl.ds(pl.multiple_of(pl.program_id(0) * width, width), width)
    right = last_ref[:, :, at].reshape(both * rows, width)
    out_ref[...] = partial_ref[:, at] + jnp.dot(left_ref[...], right, preferred_element_type=F32)
    moment_ref[...] = 0.9 * momentum_ref[...] + gradient_ref[...].astype(F32)
    size = scaled_ref.shape[0]
    scaled_ref[...] = krylov_ref[:size, :size]


def finish(partial, left, last, momentum, gradient, krylov):
    count, cols = partial.shape
    rows = momentum.shape[0]
    turns = 4
    size = STEPS * K
    vmem = pl.BlockSpec(memory_space=pltpu.VMEM)
    by_cols = pl.BlockSpec((count, cols // turns), lambda n: (0, n))
    by_rows = pl.BlockSpec((rows // turns, cols), lambda n: (n, 0))
    return pl.pallas_call(
        finish_kernel,
        grid=(turns,),
        in_specs=[vmem, vmem, vmem, by_rows, by_rows, vmem],
        out_specs=(by_cols, by_rows, pl.BlockSpec((size, size), lambda n: (0, 0))),
        out_shape=(
            jax.ShapeDtypeStruct((count, cols), F32),
            jax.ShapeDtypeStruct((rows, cols), F32),
            jax.ShapeDtypeStruct((size, size), F32),
        ),
        compiler_params=pltpu.CompilerParams(vmem_limit_bytes=24 * 1024 * 1024),
    )(partial, left, last, momentum, gradient, krylov)


def local(nf, nt, tokens, weight, momentum, gradient, probes):
    held = step_call(tokens, weight, momentum, gradient, probes, nf, nt)
    partial, last, left, krylov = (
        pltpu.with_memory_space_constraint(value, pltpu.VMEM) for value in held
    )
    return finish(partial, left, last, momentum, gradient, krylov)


def solution(mesh):
    return jax.shard_map(
        functools.partial(local, mesh.shape["fsdp"], mesh.shape["tensor"]),
        mesh=mesh,
        in_specs=(
            P("fsdp", None),
            P("fsdp", "tensor"),
            P("fsdp", "tensor"),
            P("fsdp", "tensor"),
            P(None, "tensor"),
        ),
        out_specs=(P("fsdp", "tensor"), P("fsdp", "tensor"), P()),
        check_vma=False,
    )
```

```python
import functools

import jax
import jax.numpy as jnp
from jax import lax
from jax.experimental import pallas as pl
from jax.experimental.pallas import tpu as pltpu
from jax.sharding import PartitionSpec as P

STEPS = 3
K = 32
LANES = 128
HIGHEST = lax.Precision.HIGHEST
F32 = jnp.float32


def hdot(left, right):
    return jnp.dot(left, right, precision=HIGHEST, preferred_element_type=F32)


def hdot_t(left, right):
    return lax.dot_general(
        left, right, (((1,), (1,)), ((), ())), precision=HIGHEST, preferred_element_type=F32
    )


def split(value):
    high = value.astype(jnp.bfloat16)
    rest = value - high.astype(F32)
    middle = rest.astype(jnp.bfloat16)
    return high, middle, (rest - middle.astype(F32)).astype(jnp.bfloat16)


def split_dot(left, right, contract):
    def dot(a, b):
        return lax.dot_general(a, b, (((1,), (contract,)), ((), ())), preferred_element_type=F32)

    high, middle, low = split(left)
    first = dot(jnp.concatenate([high, middle, low], axis=0), right[0])
    second = dot(jnp.concatenate([high, middle], axis=0), right[1])
    third = dot(high, right[2])
    small = first[2 * K :] + second[K:] + third
    return first[:K] + ((first[K : 2 * K] + second[:K]) + small)


def eliminate(gram):
    lane = lax.broadcasted_iota(jnp.int32, (8, LANES), 1)
    sub = lax.broadcasted_iota(jnp.int32, (8, LANES), 0)
    sub_col = lax.broadcasted_iota(jnp.int32, (8, 1), 0)
    count = K // 8
    blocks = []
    for at in range(count):
        eye = jnp.where(lane == sub + (8 * at + K), 1.0, 0.0)
        blocks.append(gram[8 * at : 8 * at + 8, :] + eye)
    for j in range(K):
        at, row = divmod(j, 8)
        pivot_row = blocks[at][row : row + 1, :]
        inverse = 1.0 / blocks[at][row : row + 1, j : j + 1]
        scaled = pivot_row * inverse
        for other in range(at, count):
            column = blocks[other][:, j : j + 1]
            if other == at:
                column = jnp.where(sub_col > row, column, 0.0)
            blocks[other] = blocks[other] - column * scaled
    upper, inverse_low = [], []
    for at in range(count):
        row = sub + 8 * at
        pivots = jnp.sum(jnp.where(lane == row, blocks[at], 0.0), axis=1, keepdims=True)
        scaled = blocks[at] / jnp.sqrt(pivots)
        upper.append(jnp.where((lane >= row) & (lane < K), scaled, 0.0))
        shifted = pltpu.roll(scaled, LANES - K, 1)
        inverse_low.append(jnp.where(lane <= row, shifted, 0.0))
    return jnp.concatenate(upper, axis=0), jnp.concatenate(inverse_low, axis=0)


def pack(square):
    tile = square[0:8, :]
    for at in range(1, K // 8):
        tile = tile + pltpu.roll(square[8 * at : 8 * at + 8, :], K * at, 1)
    return tile


def unpack(tile):
    lane = lax.broadcasted_iota(jnp.int32, (8, LANES), 1)
    parts = []
    for at in range(K // 8):
        part = tile if at == 0 else pltpu.roll(tile, LANES - K * at, 1)
        parts.append(jnp.where(lane < K, part, 0.0))
    return jnp.concatenate(parts, axis=0)


def top_value(krylov):
    def unit(power):
        return power / jnp.max(jnp.abs(power))

    power = unit(krylov)
    for turn in range(5):
        power = hdot(power, power)
        if turn == 2:
            power = unit(power)
    down = jnp.sum(power, axis=1, keepdims=True)
    along = jnp.sum(power, axis=0, keepdims=True)
    length = jnp.sqrt(jnp.sum(down * down)) * jnp.sqrt(jnp.sum(along * along))
    return jnp.sum(krylov * (down * along)) / length


def signed(n):
    return (n + 1) % 4 - 1


def mod4(at):
    return at[0] % 4, at[1] % 4


PIECES = (("a", 1), ("a", -1), ("b", 1), ("b", -1))
GROUPS = (
    ((1, 0), (0, 1)),
    ((-1, 0), (0, -1)),
    ((1, 1), (-1, -1)),
    ((1, -1), (-1, 1)),
    ((2, 0), (0, 2)),
    ((2, 1), (1, 2)),
    ((2, -1), (-1, 2)),
    ((2, 2),),
)


def onward(piece, source):
    first, sign = piece
    u, v = signed(-source[0]), signed(-source[1])
    if first == "b":
        u, v = v, u
    out = []
    if v == 0:
        if u == 0:
            out += [(1, 0), (-1, 0)]
        elif u == sign:
            out += [(sign, 0)]
        out += [(0, 1), (0, -1)]
    elif v == sign:
        out += [(0, sign)]
    if first == "b":
        out = [(v, u) for u, v in out]
    return out


def slot(at):
    i, j = mod4(at)
    return 4 * i + j


def spans(start, counts):
    out = []
    for count in counts:
        out.append((start, start + count))
        start += count
    return tuple(out)


BANDS = spans(0, (64, 64, 64, 64))


PARTNERS = sorted(
    ((i, j, other) for i in (1, 2, -1, 0) for j in (2, 1, -1, 0) for other in (0, 1) if (i, j, other) != (0, 0, 0)),
    key=lambda at: -(abs(at[0]) + abs(at[1])),
)


class Flow:
    def __init__(self, wall, rows, recv, send, sib_recv, sib_send, device_at, sibling):
        self.wall, self.rows = wall, rows
        self.recv, self.send, self.sib_recv, self.sib_send = recv, send, sib_recv, sib_send
        self.device_at, self.sibling = device_at, sibling
        self.first, self.last = rows[0][0], rows[-1][1]

    def copies(self, owner, low, high, send, recv, to):
        band = pl.ds(low, high - low)
        pltpu.make_async_remote_copy(
            src_ref=self.wall.at[owner, band],
            dst_ref=self.wall.at[owner, band],
            send_sem=send,
            recv_sem=recv,
            device_id=to,
        ).start()

    def bytes_of(self, count, high_less_low, sem):
        ref = self.wall.at[pl.ds(0, count), pl.ds(0, high_less_low)]
        return pltpu.make_async_remote_copy(
            src_ref=ref, dst_ref=ref, send_sem=sem, recv_sem=sem, device_id=self.sibling
        )

    def pass_on(self, t, owner, source, to):
        low, high = self.rows[t]
        there = self.recv.at[t, slot((source[0] - to[0], source[1] - to[1]))]
        self.copies(owner, low, high, self.send.at[t], there, self.device_at(to))

    def to_sibling(self, owner, source):
        there = self.sib_recv.at[slot((source[1], source[0]))]
        self.copies(owner, self.first, self.last, self.sib_send, there, self.sibling)

    def begin(self, owner):
        for rank in range(4):
            for t, piece in enumerate(PIECES):
                self.pass_on(t, owner, (0, 0), onward(piece, (0, 0))[rank])
        self.to_sibling(owner, (0, 0))

    def events(self, owner, source):
        for t, piece in enumerate(PIECES):
            low, high = self.rows[t]
            self.bytes_of(1, high - low, self.recv.at[t, slot(source)]).wait_recv()
            for to in onward(piece, source):
                self.pass_on(t, owner, source, to)
        self.to_sibling(owner, source)

    def last_event(self, owner, source):
        for t, (low, high) in enumerate(self.rows):
            self.bytes_of(1, high - low, self.recv.at[t, slot(source)]).wait_recv()
            there = self.sib_recv.at[slot((source[1], source[0]))]
            self.copies(owner, low, high, self.sib_send, there, self.sibling)

    def from_sibling(self, owner, source):
        self.bytes_of(1, self.last - self.first, self.sib_recv.at[slot(source)]).wait_recv()

    def sent(self):
        for t, (low, high) in enumerate(self.rows):
            self.bytes_of(15, high - low, self.send.at[t]).wait_send()
        self.bytes_of(16, self.last - self.first, self.sib_send).wait_send()


def step_kernel(
    nf,
    nt,
    tokens_ref,
    weight_hbm,
    probes_ref,
    momentum_hbm,
    gradient_hbm,
    partial_ref,
    last_ref,
    left_ref,
    krylov_ref,
    wall,
    toks,
    block,
    basis,
    small,
    weight_ref,
    momentum_ref,
    gradient_ref,
    parts,
    gbuf,
    tbuf,
    fsend,
    frecv,
    gathered,
    drecv,
    late_recv,
    late_send,
    late_sib_recv,
    late_sib_send,
    tok_sem,
    in_sem,
    left_sem,
    g_send,
    g_recv,
    t_send,
    t_recv,
    rs_send,
    rs_recv,
    ag_send,
    ag_recv,
    d_send,
    d_recv,
):
    mf = lax.axis_index("fsdp")
    mt = lax.axis_index("tensor")
    rows, cols = momentum_ref.shape
    width = cols // 8
    core = lax.rem(mf, 2)
    chip = lax.div(mf, 2)
    mx, mz = lax.div(chip, 4), lax.rem(chip, 4)

    def chip_at(at):
        i, j = at
        x = lax.rem(mx + 4 + i * (1 - core) + j * core, 4)
        z = lax.rem(mz + 4 + i * core + j * (1 - core), 4)
        return 4 * x + z

    def device_at(at):
        return {"fsdp": 2 * chip_at(at) + core}

    sibling = {"fsdp": 2 * chip + 1 - core}

    def fsdp_at(k):
        return {"fsdp": lax.rem(mf + k, nf)}

    def tensor_at(k):
        return {"tensor": lax.rem(mt + k, nt)}

    loads = [
        pltpu.make_async_copy(source, target, in_sem.at[at])
        for at, (source, target) in enumerate(
            ((momentum_hbm, momentum_ref), (gradient_hbm, gradient_ref), (weight_hbm, weight_ref))
        )
    ]
    for load in loads:
        load.start()
    barrier = pltpu.get_barrier_semaphore()

    @pl.loop(1, nf)
    def _(k):
        pl.semaphore_signal(barrier, inc=1, device_id=fsdp_at(k))

    @pl.loop(1, nt)
    def _(k):
        pl.semaphore_signal(barrier, inc=1, device_id=tensor_at(k))

    lane = lax.broadcasted_iota(jnp.int32, (K, LANES), 1)

    def to_all(src, dst, send, recv):
        for i, j, other in PARTNERS:
            to = 2 * chip_at((i, j)) + (1 - core if other else core)
            pltpu.make_async_remote_copy(
                src_ref=src(to),
                dst_ref=dst,
                send_sem=send,
                recv_sem=recv,
                device_id={"fsdp": to},
            ).start()

    def to_tensor(ref, send, recv):
        for k in (2, 1, 3):
            pltpu.make_async_remote_copy(
                src_ref=ref,
                dst_ref=ref,
                send_sem=send,
                recv_sem=recv,
                device_id=tensor_at(k),
            ).start()

    def all_of(ref, send, recv, count):
        return pltpu.make_async_remote_copy(
            src_ref=ref.at[pl.ds(0, count)],
            dst_ref=ref.at[pl.ds(0, count)],
            send_sem=send,
            recv_sem=recv,
            device_id=fsdp_at(1),
        )

    flow = Flow(wall, BANDS, late_recv, late_send, late_sib_recv, late_sib_send, device_at, sibling)

    def owner_at(source):
        return 2 * chip_at(source) + core

    block[...] = probes_ref[...]
    small[...] = jnp.zeros_like(small)

    def send_gram(step, now):
        small[:, :K] = hdot_t(now, now)
        gbuf[step, mt] = pack(small[...])
        if step == 0:
            pl.semaphore_wait(barrier, nf + nt - 2)
        to_tensor(gbuf.at[step, mt], g_send.at[step], g_recv.at[step])

    send_gram(0, probes_ref[...])
    loads[0].wait()
    loads[1].wait()
    moment = 0.9 * momentum_ref[...] + gradient_ref[...].astype(F32)
    for at, value in enumerate(split(moment)):
        parts[at] = value
    diags, uppers = [], []
    for step in range(STEPS):
        now = block[...]
        if step:
            send_gram(step, now)
        for half in range(2):
            band = slice(LANES * half, LANES * (half + 1))
            tbuf[step, mt, half] = split_dot(now, [parts[at, band] for at in range(3)], 1)
            to_tensor(tbuf.at[step, mt, half], t_send.at[step], t_recv.at[step])
        all_of(gbuf.at[step], g_send.at[step], g_recv.at[step], nt - 1).wait_recv()
        gram = gbuf[step, 0]
        for other in range(1, nt):
            gram = gram + gbuf[step, other]
        upper_next, inverse_low = eliminate(unpack(gram))
        if step:
            uppers.append(upper_next)
        all_of(tbuf.at[step], t_send.at[step], t_recv.at[step], nt - 1).wait_recv()
        total = tbuf[step, 0]
        for other in range(1, nt):
            total = total + tbuf[step, other]
        total = jnp.concatenate([total[0], total[1]], axis=1)
        inverse_low = inverse_low[:, :K]
        reduced = hdot(inverse_low, total)
        small[:, :K] = hdot_t(reduced, reduced)
        tile = pack(small[...])
        if step + 1 < STEPS:
            drecv[step, mf] = tile
            images = split_dot(reduced, parts, 0)
            for r in range(4):
                for c in range(8):
                    fsend[step, 8 * r + c] = images[
                        8 * r : 8 * r + 8, width * c : width * (c + 1)
                    ]
            frecv[step, mf] = fsend[step, mf]
            to_all(
                lambda dest: fsend.at[step, dest],
                frecv.at[step, mf],
                rs_send.at[step],
                rs_recv.at[step],
            )
            to_all(
                lambda dest: drecv.at[step, mf], drecv.at[step, mf], d_send.at[step], d_recv.at[step]
            )
            basis[step] = hdot(inverse_low, now)
            all_of(frecv.at[step], rs_send.at[step], rs_recv.at[step], nf - 1).wait_recv()
            summed = jnp.sum(frecv[step], axis=0)
            gathered[step, mf] = summed
            to_all(
                lambda dest: gathered.at[step, mf],
                gathered.at[step, mf],
                ag_send.at[step],
                ag_recv.at[step],
            )
            all_of(drecv.at[step], d_send.at[step], d_recv.at[step], nf - 1).wait_recv()
            diag = unpack(jnp.sum(drecv[step], axis=0))
            rest = hdot(diag[:, :K], basis[step])
            if step:
                rest = rest + hdot(upper_next[:, :K], basis[step - 1])
            block[...] = rest
            all_of(gathered.at[step], ag_send.at[step], ag_recv.at[step], nf - 1).wait_recv()
            for r in range(4):
                for c in range(8):
                    where = (slice(8 * r, 8 * r + 8), slice(width * c, width * (c + 1)))
                    block[where] = gathered[step, 8 * r + c] - block[where]
        else:
            drecv[step, mf] = tile
            to_all(
                lambda dest: drecv.at[step, mf], drecv.at[step, mf], d_send.at[step], d_recv.at[step]
            )
            row = lax.broadcasted_iota(jnp.int32, (K, K), 0)
            eye = jnp.where(row == lax.broadcasted_iota(jnp.int32, (K, K), 1), 1.0, 0.0)
            lows = []
            for at in range(STEPS - 1):
                small[:, :K] = hdot_t(eye, uppers[at][:, :K])
                lows.append(small[...])
            bands = [
                diags[0] + pltpu.roll(lows[0], K, 1),
                uppers[0] + pltpu.roll(diags[1], K, 1) + pltpu.roll(lows[1], 2 * K, 1),
                pltpu.roll(uppers[1], K, 1),
                jnp.zeros((K, LANES), F32),
            ]
            all_of(drecv.at[step], d_send.at[step], d_recv.at[step], nf - 1).wait_recv()
            diag = unpack(jnp.sum(drecv[step], axis=0))
            bands[2] = bands[2] + pltpu.roll(diag, 2 * K, 1)
        diags.append(diag)

    krylov = jnp.concatenate(bands, axis=0)
    top = top_value(krylov)
    krylov_ref[...] = krylov / top
    scale = 1.0 / jnp.sqrt(top)
    loads[2].wait()
    fresh = 0.9 * momentum_ref[...] + gradient_ref[...].astype(F32)
    wall[mf] = (weight_ref[...].astype(F32) - fresh * scale).astype(jnp.bfloat16)
    flow.begin(mf)

    order = [(0, 0)] + [source for group in GROUPS for source in group]

    def tokens_of(number):
        columns = pl.ds(pl.multiple_of(chip_at(order[number]) * 2 * rows, 2 * rows), 2 * rows)
        return pltpu.make_async_copy(
            tokens_ref.at[:, columns], toks.at[number % 2], tok_sem.at[number % 2]
        )

    tokens_of(0).start()
    columns = pl.ds(pl.multiple_of(chip_at(order[-1]) * 2 * rows, 2 * rows), 2 * rows)
    final = pltpu.make_async_copy(tokens_ref.at[:, columns], left_ref, left_sem)
    final.start()

    def multiply(source):
        number = order.index(source)
        if number + 2 < len(order):
            tokens_of(number + 1).start()
        left_owner = 2 * chip_at(source)
        flow.from_sibling(left_owner + 1 - core, source)
        tokens_of(number).wait()
        left = toks[number % 2]

        @pl.loop(0, cols // 1024)
        def _(n):
            at = pl.ds(pl.multiple_of(n * 1024, 1024), 1024)
            right = wall[pl.ds(left_owner, 2), :, at].reshape(2 * rows, 1024)
            product = jnp.dot(left, right, preferred_element_type=F32)
            if number:
                partial_ref[:, at] += product
            else:
                partial_ref[:, at] = product

    last = order[-1]
    for number, source in enumerate(order[1:-1]):
        flow.events(owner_at(source), source)
        if number != 1:
            multiply(order[number - (number > 1)])
    multiply(order[-3])
    multiply(order[-2])
    flow.last_event(owner_at(last), last)
    flow.from_sibling(2 * chip_at(last) + 1 - core, last)
    last_ref[...] = wall[pl.ds(2 * chip_at(last), 2)]
    final.wait()
    flow.sent()
    for step in range(STEPS):
        all_of(gbuf.at[step], g_send.at[step], g_recv.at[step], nt - 1).wait_send()
        all_of(tbuf.at[step], t_send.at[step], t_recv.at[step], nt - 1).wait_send()
        all_of(drecv.at[step], d_send.at[step], d_recv.at[step], nf - 1).wait_send()
        if step + 1 < STEPS:
            all_of(fsend.at[step], rs_send.at[step], rs_recv.at[step], nf - 1).wait_send()
            all_of(gathered.at[step], ag_send.at[step], ag_recv.at[step], nf - 1).wait_send()


def step_call(tokens, weight, momentum, gradient, probes, nf, nt):
    rows, cols = momentum.shape
    width = cols // 8
    count = tokens.shape[0]
    vmem = pl.BlockSpec(memory_space=pltpu.VMEM)
    anywhere = pl.BlockSpec(memory_space=pl.ANY)
    dma = pltpu.SemaphoreType.DMA
    return pl.pallas_call(
        functools.partial(step_kernel, nf, nt),
        out_shape=(
            pltpu.VMEM((count, cols), F32),
            pltpu.VMEM((2, rows, cols), jnp.bfloat16),
            pltpu.VMEM((count, 2 * rows), jnp.bfloat16),
            pltpu.VMEM((LANES, LANES), F32),
        ),
        in_specs=[anywhere, anywhere, vmem, anywhere, anywhere],
        out_specs=(vmem, vmem, vmem, vmem),
        scratch_shapes=[
            pltpu.VMEM((nf, rows, cols), jnp.bfloat16),
            pltpu.VMEM((2, count, 2 * rows), jnp.bfloat16),
            pltpu.VMEM((K, cols), F32),
            pltpu.VMEM((STEPS - 1, K, cols), F32),
            pltpu.VMEM((K, LANES), F32),
            pltpu.VMEM((rows, cols), jnp.bfloat16),
            pltpu.VMEM((rows, cols), F32),
            pltpu.VMEM((rows, cols), jnp.bfloat16),
            pltpu.VMEM((3, rows, cols), jnp.bfloat16),
            pltpu.VMEM((STEPS, nt, 8, LANES), F32),
            pltpu.VMEM((STEPS, nt, 2, K, LANES), F32),
            pltpu.VMEM((STEPS - 1, nf, 8, width), F32),
            pltpu.VMEM((STEPS - 1, nf, 8, width), F32),
            pltpu.VMEM((STEPS - 1, nf, 8, width), F32),
            pltpu.VMEM((STEPS, nf, 8, LANES), F32),
            dma((4, 16)),
            dma((4,)),
            dma((16,)),
            dma(()),
            dma((2,)),
            dma((3,)),
            dma(()),
            dma((STEPS,)),
            dma((STEPS,)),
            dma((STEPS,)),
            dma((STEPS,)),
            dma((STEPS - 1,)),
            dma((STEPS - 1,)),
            dma((STEPS - 1,)),
            dma((STEPS - 1,)),
            dma((STEPS,)),
            dma((STEPS,)),
        ],
        compiler_params=pltpu.CompilerParams(
            collective_id=0, has_side_effects=True, vmem_limit_bytes=48 * 1024 * 1024
        ),
    )(tokens, weight, probes, momentum, gradient)


def finish_kernel(
    partial_ref,
    left_ref,
    last_ref,
    momentum_ref,
    gradient_ref,
    krylov_ref,
    out_ref,
    moment_ref,
    scaled_ref,
):
    both, rows, cols = last_ref.shape
    width = out_ref.shape[1]
    at = pl.ds(pl.multiple_of(pl.program_id(0) * width, width), width)
    right = last_ref[:, :, at].reshape(both * rows, width)
    out_ref[...] = partial_ref[:, at] + jnp.dot(left_ref[...], right, preferred_element_type=F32)
    moment_ref[...] = 0.9 * momentum_ref[...] + gradient_ref[...].astype(F32)
    size = scaled_ref.shape[0]
    scaled_ref[...] = krylov_ref[:size, :size]


def finish(partial, left, last, momentum, gradient, krylov):
    count, cols = partial.shape
    rows = momentum.shape[0]
    turns = 4
    size = STEPS * K
    vmem = pl.BlockSpec(memory_space=pltpu.VMEM)
    by_cols = pl.BlockSpec((count, cols // turns), lambda n: (0, n))
    by_rows = pl.BlockSpec((rows // turns, cols), lambda n: (n, 0))
    return pl.pallas_call(
        finish_kernel,
        grid=(turns,),
        in_specs=[vmem, vmem, vmem, by_rows, by_rows, vmem],
        out_specs=(by_cols, by_rows, pl.BlockSpec((size, size), lambda n: (0, 0))),
        out_shape=(
            jax.ShapeDtypeStruct((count, cols), F32),
            jax.ShapeDtypeStruct((rows, cols), F32),
            jax.ShapeDtypeStruct((size, size), F32),
        ),
        compiler_params=pltpu.CompilerParams(vmem_limit_bytes=24 * 1024 * 1024),
    )(partial, left, last, momentum, gradient, krylov)


def local(nf, nt, tokens, weight, momentum, gradient, probes):
    held = step_call(tokens, weight, momentum, gradient, probes, nf, nt)
    partial, last, left, krylov = (
        pltpu.with_memory_space_constraint(value, pltpu.VMEM) for value in held
    )
    return finish(partial, left, last, momentum, gradient, krylov)


def solution(mesh):
    return jax.shard_map(
        functools.partial(local, mesh.shape["fsdp"], mesh.shape["tensor"]),
        mesh=mesh,
        in_specs=(
            P("fsdp", None),
            P("fsdp", "tensor"),
            P("fsdp", "tensor"),
            P("fsdp", "tensor"),
            P(None, "tensor"),
        ),
        out_specs=(P("fsdp", "tensor"), P("fsdp", "tensor"), P()),
        check_vma=False,
    )
```
